32 devices in a mesh: amp: 4 (over y, core), own: 8 (over z, x).
Axes of the slice: x: 2, y: 2, z: 4, core: 2. Of those that a mesh axis runs over, the one named last changes fastest.
Arguments:
- amplitudes: bfloat16 [32, 2304, 192], P('own', None, 'amp'), may hold values from -6 to 6
- integrals: bfloat16 [32, 1152, 2304], P('own'), as said below
- occ_irrep: int32 [34], replicated, may hold values from 0 to 7, as said below
- tile_irrep: int32 [18], replicated, may hold values from 0 to 7, as said below
Outputs:
- cycle_term: bfloat16 [2304, 2304], P(('amp', 'own'))
The draws below stay inside these ranges and needn't reach their ends.
Inputs may be any that keep to these rules, and one draw needn't show every extreme that they name: `occ_irrep`: labels of the D2h group, combined by XOR; every label occurs, and all labels occur equally often up to one. `tile_irrep`: labels of the D2h group, combined by XOR; every label occurs, and all labels occur equally often up to one, so some label has exactly 3 tiles. integrals[k, c, (j, b)] is zero unless the labels of k, c, j and b combine by XOR to 0.
All inputs are finite; a program needn't handle non-finite values.
Results may differ from the reference program's by a relative error of at most 0.001.
Values may be sent and summed in bfloat16 or wider, within the bound.
A program may use at most 128 MiB of HBM per device.

```python
import jax
import jax.numpy as jnp
from jax import lax

V = 1152
TILE = 64
SLOTS = 3
NI = 2
NK = 32


def occ_labels(key):
    order = jax.random.permutation(jax.random.fold_in(key, 11), NI + NK)
    return (order % 8).astype(jnp.int32)


def tile_labels(key):
    order = jax.random.permutation(jax.random.fold_in(key, 23), V // TILE)
    return (order % 8).astype(jnp.int32)


def draw_occ_irrep(key, part):
    return occ_labels(key)


def draw_tile_irrep(key, part):
    return tile_labels(key)


def draw_integrals(key, part):
    occ = occ_labels(key)
    virt_lab = jnp.repeat(tile_labels(key), TILE)
    slab_lab = jnp.bitwise_xor(jnp.repeat(occ[:NI], V), jnp.tile(virt_lab, NI))
    k_lab = occ[NI:]
    values = jax.random.normal(jax.random.fold_in(key, 37), (NK, V, NI * V), jnp.float32)
    values = values * (NK * V / 8.0) ** (-0.5)
    labels = jnp.bitwise_xor(jnp.bitwise_xor(k_lab[:, None, None], virt_lab[None, :, None]), slab_lab[None, None, :])
    return jnp.where(labels == 0, values, jnp.zeros((), jnp.float32)).astype(jnp.bfloat16)


def raised(values, own_key, source, target, blocks, factor):
    def block_of(axis_at):
        return (jnp.arange(values.shape[axis_at]) // (values.shape[axis_at] // blocks)).reshape((-1,) + (1,) * (values.ndim - 1 - axis_at))

    near = jax.random.permutation(own_key, blocks)[block_of(target)]
    far = (block_of(target) + blocks // 2) % blocks
    return jnp.where((block_of(source) == near) | (block_of(source) == far), factor * values, values)


def level_of(key, dims, cuts, least, largest):
    def one(axis_at, parts):
        draws = jax.random.uniform(jax.random.fold_in(jax.random.fold_in(key, 6), axis_at), (parts,), jnp.float32, least / len(cuts), largest / len(cuts))
        return jnp.repeat(jnp.exp(draws), dims[axis_at] // parts).reshape((-1,) + (1,) * (len(dims) - axis_at - 1))

    factor_of = one(*cuts[0])
    for cut in cuts[1:]:
        factor_of = factor_of * one(*cut)
    return factor_of


def heavy_noise(own_key, shape, spread, most, cuts, heavy, kind=jnp.bfloat16):
    drawn = spread * jax.random.normal(own_key, shape, jnp.float32)
    if cuts:
        drawn = drawn * level_of(own_key, shape, cuts, -0.22, 0.18)
    return jnp.clip(raised(drawn, jax.random.fold_in(own_key, 3), *heavy), -most, most).astype(kind)


def setup_inputs(seed: int = 0) -> dict:
    key_of = jax.random.split(jax.random.key(seed), 5)
    return {
        "amplitudes": heavy_noise(key_of[0], (NK, NI * V, SLOTS * TILE), 1.0, 6.0, ((0, 8), (2, 4)), (0, 1, 8, 2.0)),
        "integrals": draw_integrals(jax.random.fold_in(key_of[4], 71), 0),
        "occ_irrep": draw_occ_irrep(jax.random.fold_in(key_of[4], 71), 0),
        "tile_irrep": draw_tile_irrep(jax.random.fold_in(key_of[4], 71), 0),
    }


def tile_ranks(tile_irrep):
    count = tile_irrep.shape[0]
    index = jnp.arange(count, dtype=jnp.int32)
    same = (tile_irrep[:, None] == tile_irrep[None, :]) & (index[None, :] < index[:, None])
    return jnp.sum(same.astype(jnp.int32), axis=1).astype(jnp.int32)


def unpack(packed, wanted, tile_irrep, ranks):
    slot_ids = jnp.arange(SLOTS, dtype=jnp.int32)
    select = (tile_irrep[None, None, :] == wanted[:, None, None]) & (ranks[None, None, :] == slot_ids[None, :, None])
    pieces = packed.astype(jnp.float32).reshape(packed.shape[0], SLOTS, TILE)
    dense = jnp.einsum("rjt,rje->rte", select.astype(jnp.float32), pieces)
    return dense.reshape(packed.shape[0], V).astype(jnp.bfloat16)


def reference(amplitudes, integrals, occ_irrep, tile_irrep):
    virt_lab = jnp.repeat(tile_irrep, TILE)
    row_lab = jnp.bitwise_xor(jnp.repeat(occ_irrep[:NI], V), jnp.tile(virt_lab, NI))
    k_labels = occ_irrep[NI:]
    ranks = tile_ranks(tile_irrep)

    def accumulate(total, items):
        block, weights, k_label = items
        dense = unpack(block, jnp.bitwise_xor(row_lab, k_label), tile_irrep, ranks)
        return total + jnp.dot(dense, weights, preferred_element_type=jnp.float32), None

    start = jnp.zeros((NI * V, NI * V), jnp.float32)
    cycle = lax.scan(accumulate, start, (amplitudes, integrals, k_labels))[0]
    return (cycle + cycle.T).astype(jnp.bfloat16)
```

```python
import functools
import itertools

import jax
import jax.numpy as jnp
from jax import lax
from jax.experimental import pallas as pl
from jax.experimental.pallas import tpu as pltpu
from jax.sharding import PartitionSpec as P

TILE = 64
NI = 2
LABELS = 8
LANES = 128
LEVELS = 32767.0
LEAST = 1e-30
MESH = pl.DeviceIdType.MESH


def gcd(a, b):
    return a if b == 0 else gcd(b, a % b)


def local_kernel(n_tiles, slots, amp_ref, int_ref, occ_hbm, tile_hbm, out_ref, w_ref, occ_ref, tile_ref, tile_of, row_of, count, local_sems, sems):
    k_local, width, rows = amp_ref.shape
    pieces, grain = w_ref.shape[2], w_ref.shape[3]
    wide = NI * slots
    amp_index = lax.axis_index("amp")
    own_index = lax.axis_index("own")

    occ_copy = pltpu.make_async_copy(occ_hbm, occ_ref, local_sems.at[1])
    tile_copy = pltpu.make_async_copy(tile_hbm, tile_ref, local_sems.at[2])
    tile_copy.start()
    occ_copy.start()

    for i in range(LABELS):
        count[i] = 0
        for s in range(slots):
            tile_of[i * slots + s] = -1
        for q in range(wide):
            row_of[i * wide + q] = -1
    tile_copy.wait()
    for t in range(n_tiles):
        lab = tile_ref[t]
        rank = count[lab]
        tile_of[lab * slots + rank] = t
        count[lab] = rank + 1

    def copy_of(lab, j):
        at = amp_index * width + j * grain
        t = tile_of[lab * slots + at // TILE]
        start = pl.multiple_of(jnp.maximum(t, 0) * TILE + at % TILE, grain)
        copy = pltpu.make_async_copy(int_ref.at[:, pl.ds(start, grain), :], w_ref.at[lab, :, j], sems.at[lab, j])
        return t, copy

    for lab in range(LABELS):
        for j in range(pieces):
            t, copy = copy_of(lab, j)

            @pl.when(t >= 0)
            def _():
                copy.start()

            @pl.when(t < 0)
            def _():
                w_ref[lab, :, j] = jnp.zeros((k_local, grain, rows), w_ref.dtype)

    for i in range(LABELS):
        count[i] = 0
    occ_copy.wait()
    for u in range(NI * n_tiles):
        lab = jnp.bitwise_xor(occ_ref[u // n_tiles], tile_ref[u % n_tiles])
        rank = count[lab]
        row_of[lab * wide + rank] = u
        count[lab] = rank + 1

    k_lab = [occ_ref[NI + own_index * k_local + k] for k in range(k_local)]

    for lab in range(LABELS):
        for j in range(pieces):
            t, copy = copy_of(lab, j)

            @pl.when(t >= 0)
            def _():
                copy.wait()

    low = lax.broadcasted_iota(jnp.int32, (width, LANES), 1) < TILE

    def block(lab, carry):
        tiles = [jnp.maximum(row_of[lab * wide + q], 0) for q in range(wide)]
        lanes = [pl.ds(pl.multiple_of(u // 2 * LANES, LANES), LANES) for u in tiles]

        def gather(load):
            turned = [pltpu.roll(load(at), (u + q) % 2 * TILE, 1) for q, (at, u) in enumerate(zip(lanes, tiles))]
            return jnp.concatenate([jnp.where(low, *turned[q : q + 2]) for q in range(0, wide, 2)], axis=1)

        a = [gather(lambda at: amp_ref[k, :, at]) for k in range(k_local)]
        w = [
            gather(lambda at: w_ref[jnp.bitwise_xor(lab, k_lab[k]), k, :, :, at].reshape(width, LANES))
            for k in range(k_local)
        ]
        s = lax.dot_general(
            jnp.concatenate(a + w, axis=0),
            jnp.concatenate(w + a, axis=0),
            (((0,), (0,)), ((), ())),
            preferred_element_type=jnp.float32,
        )
        for q in range(wide):
            u = row_of[lab * wide + q]

            @pl.when(u >= 0)
            def _():
                for c in range(out_ref.shape[0]):
                    out_ref[c, pl.ds(pl.multiple_of(u * TILE, TILE), TILE), :] = s[
                        q * TILE : (q + 1) * TILE, c * LANES : (c + 1) * LANES
                    ]

        return carry

    lax.fori_loop(0, LABELS, block, 0)


def split_of(n_amp, n_own):
    lo = 2 if n_own <= 8 else 8
    return n_amp // 2, n_own // lo, lo


def scatter_kernel(x_ref, occ_ref, tile_ref, out_ref, near_ref, fin_ref, lab_ref, rank_ref, near_send, near_recv, *scratch):
    chunks, n_y, _, n_hi, n_lo, share, _ = x_ref.shape
    amp, own = lax.axis_index("amp"), lax.axis_index("own")
    y, core, hi, lo = amp // 2, amp % 2, own // n_lo, own % n_lo
    sizes = (n_y * n_lo, n_hi)
    planes = [(0, 1) if c < 2 else (1, 0) for c in range(chunks)]
    bufs = [scratch[c * 12 : (c + 1) * 12] for c in range(chunks)]

    def device_of(flat, high, flip=0):
        y_at, lo_at, hi_at = (y + flat // n_lo) % n_y, (lo + flat % n_lo) % n_lo, (hi + high) % n_hi
        return y_at, lo_at, hi_at

    def id_of(flat, high):
        y_at, lo_at, hi_at = device_of(flat, high)
        return (y_at * 2 + core, hi_at * n_lo + lo_at)

    def away(kind, j):
        return id_of(j, 0) if kind == 0 else id_of(0, j)

    def toward(kind, j):
        if kind == 1:
            return id_of(0, n_hi - j)
        return id_of((n_y - j // n_lo) % n_y * n_lo + (n_lo - j % n_lo) % n_lo, 0)

    other = (y * 2 + 1 - core, own)
    barrier = pltpu.get_barrier_semaphore()
    pl.semaphore_signal(barrier, inc=1, device_id=other, device_id_type=MESH)
    for kind in range(2):
        for j in range(1, sizes[kind]):
            pl.semaphore_signal(barrier, inc=1, device_id=toward(kind, j), device_id_type=MESH)
    pl.semaphore_wait(barrier, 1 + sizes[0] - 1 + sizes[1] - 1)

    def near(c):
        return pltpu.make_async_remote_copy(
            src_ref=x_ref.at[c, :, 1 - core],
            dst_ref=near_ref.at[c],
            send_sem=near_send.at[c],
            recv_sem=near_recv.at[c],
            device_id=other,
            device_id_type=MESH,
        )

    def copies(c, s, j):
        q_send, q_recv, m_send, m_recv, send, recv = bufs[c][6 * s : 6 * s + 6]
        return [
            pltpu.make_async_remote_copy(
                src_ref=src.at[j - 1],
                dst_ref=dst.at[j - 1],
                send_sem=send.at[which, j - 1],
                recv_sem=recv.at[which, j - 1],
                device_id=away(planes[c][s], j),
                device_id_type=MESH,
            )
            for which, (src, dst) in enumerate(((m_send, m_recv), (q_send, q_recv)))
        ]

    def pair(c, j, i):
        y_at, lo_at, hi_at = device_of(*((j, i) if planes[c][0] == 0 else (i, j)))
        return x_ref[c, y_at, core, hi_at, lo_at] + near_ref[c, y_at, hi_at, lo_at]

    def coded(x):
        most = jnp.maximum(jnp.max(jnp.abs(x), axis=0, keepdims=True), LEAST)
        return jnp.round(x * (LEVELS / most)).astype(jnp.int32).astype(jnp.int16), most * (1.0 / LEVELS)

    def plain(q, m):
        return q.astype(jnp.int32).astype(jnp.float32) * m

    def first(c):
        n, inner = (sizes[k] for k in planes[c])
        q_send, _, m_send = bufs[c][:3]
        for j in range(1, n):

            def step(i, carry):
                q_send[j - 1, i], m_send[j - 1, i] = coded(pair(c, j, i))
                return carry

            lax.fori_loop(0, inner, step, 0)
            for copy in copies(c, 0, j):
                copy.start()

    def total(c, i):
        n = sizes[planes[c][0]]
        _, q_recv, _, m_recv = bufs[c][:4]
        x = pair(c, 0, i)
        for j in range(1, n):
            x = x + plain(q_recv[j - 1, i], m_recv[j - 1, i])
        return x

    def second(c):
        n = sizes[planes[c][1]]
        q_send, _, m_send = bufs[c][6:9]
        for j in range(1, n):
            q_send[j - 1], m_send[j - 1] = coded(total(c, j))
            for copy in copies(c, 1, j):
                copy.start()
        fin_ref[c] = total(c, 0)

    def last(c):
        n = sizes[planes[c][1]]
        _, q_recv, _, m_recv = bufs[c][6:10]
        x = fin_ref[c]
        for j in range(1, n):
            x = x + plain(q_recv[j - 1], m_recv[j - 1])
        fin_ref[c] = x

    def received(c, s):
        for j in range(1, sizes[planes[c][s]]):
            for copy in copies(c, s, j):
                copy.wait_recv()

    for c in range(chunks):
        near(c).start()
    n_tiles = tile_ref.shape[0]
    labs = [jnp.bitwise_xor(occ_ref[u // n_tiles], tile_ref[u % n_tiles]) for u in range(NI * n_tiles)]
    for u, lab in enumerate(labs):
        lab_ref[u] = lab
        rank = jnp.int32(0)
        for same in labs[:u]:
            rank = rank + jnp.where(same == lab, 1, 0)
        rank_ref[u] = rank
    for c in range(chunks):
        near(c).wait_recv()
        first(c)
    for c in range(chunks):
        received(c, 0)
        second(c)
    for c in range(chunks):
        received(c, 1)
        last(c)
    for c in range(chunks):
        near(c).wait_send()
        for s in range(2):
            for j in range(1, sizes[planes[c][s]]):
                for copy in copies(c, s, j):
                    copy.wait_send()
    expand((amp * lax.axis_size("own") + own) * share, fin_ref, lab_ref, rank_ref, out_ref)


def expand(base, x_ref, lab_ref, rank_ref, out_ref):
    share = x_ref.shape[1]
    count = lab_ref.shape[0]
    first = base // TILE
    row = base + lax.broadcasted_iota(jnp.int32, (share, LANES), 0)
    low = lax.broadcasted_iota(jnp.int32, (share, LANES), 1) < TILE
    row_lab = jnp.where(row < (first + 1) * TILE, lab_ref[first], lab_ref[jnp.minimum(first + 1, count - 1)])
    for u in range(0, count, 2):
        ranks = [rank_ref[u + h] for h in range(2)]
        turned = [pltpu.roll(x_ref[jnp.minimum(rank // 2, x_ref.shape[0] - 1)], (rank + h) % 2 * TILE, 1) for h, rank in enumerate(ranks)]
        match = row_lab == jnp.where(low, lab_ref[u], lab_ref[u + 1])
        out_ref[:, u * TILE : (u + 2) * TILE] = jnp.where(match, jnp.where(low, *turned), 0.0).astype(out_ref.dtype)


def shards(amplitudes, integrals, occ_irrep, tile_irrep):
    n_amp = lax.axis_size("amp")
    n_own = lax.axis_size("own")
    k_local, rows, width = amplitudes.shape
    n_tiles = tile_irrep.shape[0]
    slots = width * n_amp // TILE
    grain = gcd(width, TILE)
    chunks = NI * slots * TILE // LANES
    vmem, smem, hbm = (pl.BlockSpec(memory_space=m) for m in (pltpu.VMEM, pltpu.SMEM, pltpu.HBM))
    packed = pl.pallas_call(
        functools.partial(local_kernel, n_tiles, slots),
        out_shape=jax.ShapeDtypeStruct((chunks, rows, LANES), jnp.float32),
        in_specs=[vmem] + [hbm] * 3,
        out_specs=vmem,
        scratch_shapes=[
            pltpu.VMEM((LABELS, k_local, width // grain, grain, rows), jnp.bfloat16),
            pltpu.SMEM(occ_irrep.shape, jnp.int32),
            pltpu.SMEM(tile_irrep.shape, jnp.int32),
            pltpu.SMEM((LABELS * slots,), jnp.int32),
            pltpu.SMEM((LABELS * NI * slots,), jnp.int32),
            pltpu.SMEM((LABELS,), jnp.int32),
            pltpu.SemaphoreType.DMA((3,)),
            pltpu.SemaphoreType.DMA((LABELS, width // grain)),
        ],
        compiler_params=pltpu.CompilerParams(vmem_limit_bytes=40 * 2**20),
        name="local",
    )(jnp.swapaxes(amplitudes, 1, 2), integrals, occ_irrep, tile_irrep)

    share = rows // (n_amp * n_own)
    n_y, n_hi, n_lo = split_of(n_amp, n_own)
    scratch = []
    for c in range(chunks):
        for s in range(2):
            n, inner = (n_y * n_lo, n_hi) if (c < 2) == (s == 0) else (n_hi, n_y * n_lo)
            lead = (n - 1, inner) if s == 0 else (n - 1,)
            scratch += [pltpu.VMEM(lead + (share, LANES), jnp.int16)] * 2
            scratch += [pltpu.VMEM(lead + (1, LANES), jnp.float32)] * 2
            scratch += [pltpu.SemaphoreType.DMA((2, n - 1))] * 2
    return pl.pallas_call(
        scatter_kernel,
        out_shape=jax.ShapeDtypeStruct((share, rows), jnp.bfloat16),
        in_specs=[vmem, smem, smem],
        out_specs=vmem,
        scratch_shapes=[
            pltpu.VMEM((chunks, n_y, n_hi, n_lo, share, LANES), jnp.float32),
            pltpu.VMEM((chunks, share, LANES), jnp.float32),
            pltpu.SMEM((NI * n_tiles,), jnp.int32),
            pltpu.SMEM((NI * n_tiles,), jnp.int32),
            pltpu.SemaphoreType.DMA((chunks,)),
            pltpu.SemaphoreType.DMA((chunks,)),
        ]
        + scratch,
        compiler_params=pltpu.CompilerParams(collective_id=0, has_side_effects=True, vmem_limit_bytes=40 * 2**20),
        name="scatter",
    )(packed.reshape((chunks, n_y, 2, n_hi, n_lo, share, LANES)), occ_irrep, tile_irrep)


def solution(mesh):
    return jax.shard_map(
        shards,
        mesh=mesh,
        in_specs=(P("own", None, "amp"), P("own", None, None), P(), P()),
        out_specs=P(("amp", "own"), None),
        check_vma=False,
    )
```

```python
import functools

import jax
import jax.numpy as jnp
from jax import lax
from jax.experimental import pallas as pl
from jax.experimental.pallas import tpu as pltpu
from jax.sharding import PartitionSpec as P

TILE = 64
NI = 2
LABELS = 8
LANES = 128
LEVELS = 32767.0
LEAST = 1e-30
MESH = pl.DeviceIdType.MESH
AHEAD = 3


def gcd(a, b):
    return a if b == 0 else gcd(b, a % b)


def pack_kernel(n_tiles, slots, amp_hbm, int_hbm, occ_hbm, tile_hbm, a_ref, w_ref, amp_ref, int_ref, turn_ref, occ_ref, tile_ref, tile_of, count, small_sems, sems):
    k_local, width, rows = amp_ref.shape
    pieces, grain = int_ref.shape[2], int_ref.shape[3]
    depth = a_ref.shape[2]
    amp_index = lax.axis_index("amp")
    own_index = lax.axis_index("own")

    tile_copy = pltpu.make_async_copy(tile_hbm, tile_ref, small_sems.at[0])
    occ_copy = pltpu.make_async_copy(occ_hbm, occ_ref, small_sems.at[1])
    amp_copy = pltpu.make_async_copy(amp_hbm, amp_ref, small_sems.at[2])
    tile_copy.start()
    occ_copy.start()
    amp_copy.start()
    for i in range(LABELS):
        count[i] = 0
        for s in range(slots):
            tile_of[i * slots + s] = -1
    tile_copy.wait()
    for t in range(n_tiles):
        lab = tile_ref[t]
        rank = count[lab]
        tile_of[lab * slots + rank] = t
        count[lab] = rank + 1
    occ_copy.wait()
    k_lab = [occ_ref[NI + own_index * k_local + k] for k in range(k_local)]

    def copies_of(lab):
        for k in range(k_local):
            for j in range(pieces):
                at = amp_index * width + j * grain
                t = tile_of[jnp.bitwise_xor(lab, k_lab[k]) * slots + at // TILE]
                start = pl.multiple_of(jnp.maximum(t, 0) * TILE + at % TILE, grain)
                copy = pltpu.make_async_copy(int_hbm.at[k, pl.ds(start, grain), :], int_ref.at[lab, k, j], sems.at[lab, k, j])
                yield k, j, t, copy

    def fetch(lab):
        for k, j, t, copy in copies_of(lab):

            @pl.when(t >= 0)
            def _():
                copy.start()

            @pl.when(t < 0)
            def _():
                int_ref[lab, k, j] = jnp.zeros((grain, rows), int_ref.dtype)

    def turned(parts):
        spare = depth - k_local * width
        if spare:
            parts = parts + [jnp.zeros((spare, LANES), a_ref.dtype)]
        return jnp.concatenate(parts, axis=0).T

    for lab in range(AHEAD):
        fetch(lab)
    amp_copy.wait()

    def turn(m, carry):
        at = pl.ds(pl.multiple_of(m * LANES, LANES), LANES)
        turn_ref[at, :] = turned([amp_ref[k, :, at] for k in range(k_local)])
        return carry

    lax.fori_loop(0, rows // LANES, turn, 0)

    def block(lab, carry):
        @pl.when(lab < LABELS - AHEAD)
        def _():
            fetch(lab + AHEAD)

        for _, _, t, copy in copies_of(lab):

            @pl.when(t >= 0)
            def _():
                copy.wait()

        for q in range(NI * slots):
            i, j = q // slots, q % slots
            t = tile_of[jnp.bitwise_xor(lab, occ_ref[i]) * slots + j]
            u = i * n_tiles + jnp.maximum(t, 0)
            to = pl.ds(q * TILE, TILE)
            a_ref[lab, to, :] = turn_ref[pl.ds(pl.multiple_of(u * TILE, TILE), TILE), :]
            at = pl.ds(pl.multiple_of(u // 2 * LANES, LANES), LANES)
            w = turned([int_ref[lab, k, :, :, at].reshape(width, LANES) for k in range(k_local)])
            w_ref[lab, to, :] = jnp.where(u % 2 == 0, w[:TILE], w[TILE:])
        return carry

    lax.fori_loop(0, LABELS, block, 0)


def split_of(n_amp, n_own):
    lo = 2 if n_own <= 8 else 8
    return n_amp // 2, n_own // lo, lo


def cycle_kernel(n_y, n_hi, n_lo, slots, a_ref, w_ref, occ_hbm, tile_hbm, out_ref, s_ref, x_ref, near_q, near_got, near_m, near_got_m, fin_ref, occ_ref, tile_ref, rank_ref, small_sems, near_send, near_recv, *bufs):
    n_own = n_hi * n_lo
    share = fin_ref.shape[1]
    n_tiles = tile_ref.shape[0]
    half = slots * TILE
    wide = NI * half
    amp, own = lax.axis_index("amp"), lax.axis_index("own")
    y, core, hi, lo = amp // 2, amp % 2, own // n_lo, own % n_lo
    n_flat = n_y * n_lo
    split = wide - LANES
    parts = [(0, split), (split, wide)]
    other = (y * 2 + 1 - core, own)

    def at_of(flat, high):
        return (y + flat // n_lo) % n_y, (hi + high) % n_hi, (lo + flat % n_lo) % n_lo

    def id_of(flat, high):
        y_at, hi_at, lo_at = at_of(flat, high)
        return (y_at * 2 + core, hi_at * n_lo + lo_at)

    tile_copy = pltpu.make_async_copy(tile_hbm, tile_ref, small_sems.at[0])
    occ_copy = pltpu.make_async_copy(occ_hbm, occ_ref, small_sems.at[1])
    tile_copy.start()
    occ_copy.start()
    barrier = pltpu.get_barrier_semaphore()
    pl.semaphore_signal(barrier, inc=1, device_id=other, device_id_type=MESH)
    for j in range(1, n_flat):
        back = (n_y - j // n_lo) % n_y * n_lo + (n_lo - j % n_lo) % n_lo
        pl.semaphore_signal(barrier, inc=1, device_id=id_of(back, 0), device_id_type=MESH)
    for j in range(1, n_hi):
        pl.semaphore_signal(barrier, inc=1, device_id=id_of(0, n_hi - j), device_id_type=MESH)

    def coded(x):
        most = jnp.maximum(jnp.max(jnp.abs(x), axis=0, keepdims=True), LEAST)
        return jnp.round(x * (LEVELS / most)).astype(jnp.int32).astype(jnp.int16), most * (1.0 / LEVELS)

    def plain(q, m):
        return q.astype(jnp.int32).astype(jnp.float32) * m

    def remote(src, dst, send, recv, to):
        return pltpu.make_async_remote_copy(src_ref=src, dst_ref=dst, send_sem=send, recv_sem=recv, device_id=to, device_id_type=MESH)

    def near(y_at):
        return [
            remote(src.at[y_at], dst.at[y_at], near_send.at[which, y_at], near_recv.at[which, y_at], other)
            for which, (src, dst) in enumerate(((near_m, near_got_m), (near_q, near_got)))
        ]

    def block(y_at, core_at, own_at, lanes):
        at = core_at * n_own + own_at
        if len(x_ref.shape) == 4:
            return x_ref[y_at, at, :, lanes]
        return x_ref[y_at, pl.ds(pl.multiple_of(at * share, 8), share), lanes]

    def multiply(i):
        rows = pl.ds(pl.multiple_of(i * half, TILE), half)
        over = (((1,), (1,)), ((), ()))

        def step(lab, carry):
            s = lax.dot_general(a_ref[lab, rows, :], w_ref[lab], over, preferred_element_type=jnp.float32)
            s = s + lax.dot_general(w_ref[lab, rows, :], a_ref[lab], over, preferred_element_type=jnp.float32)
            s_ref[lab] = s.reshape(s_ref.shape[1:])
            return carry

        lax.fori_loop(0, LABELS, step, 0)

    def spread(y_at, i):
        count = NI * n_tiles // n_y
        for n in range(count):
            t = y_at * count + n - i * n_tiles
            lab = jnp.bitwise_xor(occ_ref[i], tile_ref[t])
            rank = rank_ref[t]
            if len(x_ref.shape) == 3:
                x_ref[y_at, n * TILE : (n + 1) * TILE] = s_ref[lab, rank]
                continue
            tile = s_ref[lab, rank]
            for b in range(n * TILE // share, -(-(n + 1) * TILE // share)):
                low, high = max(n * TILE, b * share), min((n + 1) * TILE, (b + 1) * share)
                x_ref[y_at, b, low - b * share : high - b * share] = tile[low - n * TILE : high - n * TILE]

        def step(b, carry):
            near_q[y_at, b], near_m[y_at, b] = coded(block(y_at, 1 - core, b, slice(None)))
            return carry

        lax.fori_loop(0, n_own, step, 0)

    def pair(p, flat, high):
        y_at, hi_at, lo_at = at_of(flat, high)
        own_at = hi_at * n_lo + lo_at
        lanes = slice(*parts[p])
        return block(y_at, core, own_at, lanes) + plain(near_got[y_at, own_at, :, lanes], near_got_m[y_at, own_at, :, lanes])

    def far(p, s, j, stage):
        q_send, q_got, m_send, m_got, send, recv = bufs[12 * p + 6 * s :][:6]
        to = id_of(j, 0) if p == s else id_of(0, j)
        at = (j - 1,)
        if p == 1 and s == 0:
            at = (j - 1, pl.ds(stage[0] * n_lo, len(stage) * n_lo))
        where = stage[0] if p == 1 and s == 0 else 0
        return [
            remote(src.at[at], dst.at[at], send.at[which, j - 1, where], recv.at[which, j - 1, where], to)
            for which, (src, dst) in enumerate(((m_send, m_got), (q_send, q_got)))
        ]

    def first(p, stage):
        q_send, _, m_send = bufs[12 * p :][:3]
        if p == 0:
            for j in range(stage[0] * n_lo, (stage[-1] + 1) * n_lo):
                if j == 0:
                    continue

                def step(h, carry):
                    q_send[j - 1, h], m_send[j - 1, h] = coded(pair(p, j, h))
                    return carry

                lax.fori_loop(0, n_hi, step, 0)
                for copy in far(p, 0, j, stage):
                    copy.start()
        else:
            for j in range(1, n_hi):
                for flat in range(stage[0] * n_lo, (stage[-1] + 1) * n_lo):
                    q_send[j - 1, flat], m_send[j - 1, flat] = coded(pair(p, flat, j))
                for copy in far(p, 0, j, stage):
                    copy.start()

    def total(p, i):
        _, q_got, _, m_got = bufs[12 * p :][:4]
        x = pair(p, 0, i) if p == 0 else pair(p, i, 0)
        for j in range(q_got.shape[0]):
            x = x + plain(q_got[j, i], m_got[j, i])
        return x

    def keep(p, x):
        for c in range((parts[p][1] - parts[p][0]) // LANES):
            fin_ref[parts[p][0] // LANES + c] = x[:, c * LANES : (c + 1) * LANES]

    def second(p):
        q_send, _, m_send = bufs[12 * p + 6 :][:3]
        for j in range(1, q_send.shape[0] + 1):
            q_send[j - 1], m_send[j - 1] = coded(total(p, j))
            for copy in far(p, 1, j, None):
                copy.start()
        return total(p, 0)

    def last(p, x):
        _, q_got, _, m_got = bufs[12 * p + 6 :][:4]
        for j in range(q_got.shape[0]):
            x = x + plain(q_got[j], m_got[j])
        keep(p, x)

    if n_y == 2:
        stages = [([1], [(1 - y, 1 - y)]), ([0], [(y, y)])]
    else:
        stages = [(list(range(n_y)), [(y_at, y_at * NI // n_y) for y_at in range(n_y)])]

    done = None
    ready = False
    for _, work in stages:
        for y_at, i in work:
            if done is None or n_y == 2 or done != i:
                multiply(i)
                done = i
            if not ready:
                ready = True
                tile_copy.wait()
                occ_copy.wait()
                for t in range(n_tiles):
                    rank = jnp.int32(0)
                    for before in range(t):
                        rank = rank + jnp.where(tile_ref[before] == tile_ref[t], 1, 0)
                    rank_ref[t] = jnp.minimum(rank, slots - 1)
                spread(y_at, i)
                pl.semaphore_wait(barrier, n_flat + n_hi - 1)
            else:
                spread(y_at, i)
            for copy in near(y_at):
                copy.start()
    for stage, work in stages:
        for y_at, _ in work:
            for copy in near(y_at):
                copy.wait_recv()
        for p in range(2):
            first(p, stage)

    def received(p, s):
        for stage in [stage for stage, _ in stages] if s == 0 else [None]:
            for j in sent(p, s, stage):
                for copy in far(p, s, j, stage):
                    copy.wait_recv()

    def sent(p, s, stage):
        if p == 0 and s == 0:
            return [j for j in range(stage[0] * n_lo, (stage[-1] + 1) * n_lo) if j]
        return range(1, n_flat if p == s else n_hi)

    kept = []
    for p in range(2):
        received(p, 0)
        kept.append(second(p))
    for p in range(2):
        received(p, 1)
        last(p, kept[p])
    for _, work in stages:
        for y_at, _ in work:
            for copy in near(y_at):
                copy.wait_send()
    for p in range(2):
        for s in range(2):
            for stage in [stage for stage, _ in stages] if s == 0 else [None]:
                for j in sent(p, s, stage):
                    for copy in far(p, s, j, stage):
                        copy.wait_send()
    expand((amp * n_own + own) * share, slots, fin_ref, occ_ref, tile_ref, rank_ref, out_ref)


def expand(base, slots, x_ref, occ_ref, tile_ref, rank_ref, out_ref):
    share = x_ref.shape[1]
    n_tiles = tile_ref.shape[0]
    count = NI * n_tiles
    labs = [jnp.bitwise_xor(occ_ref[u // n_tiles], tile_ref[u % n_tiles]) for u in range(count)]

    def label(u):
        return jnp.bitwise_xor(occ_ref[u // n_tiles], tile_ref[u % n_tiles])

    first = base // TILE
    row = base + lax.broadcasted_iota(jnp.int32, (share, LANES), 0)
    low = lax.broadcasted_iota(jnp.int32, (share, LANES), 1) < TILE
    row_lab = jnp.where(row < (first + 1) * TILE, label(first), label(jnp.minimum(first + 1, count - 1)))
    for u in range(0, count, 2):
        slot = [(u + h) // n_tiles * slots + rank_ref[(u + h) % n_tiles] for h in range(2)]
        turned = [pltpu.roll(x_ref[at // 2], (at + h) % 2 * TILE, 1) for h, at in enumerate(slot)]
        match = row_lab == jnp.where(low, labs[u], labs[u + 1])
        out_ref[:, u * TILE : (u + 2) * TILE] = jnp.where(match, jnp.where(low, *turned), 0.0).astype(out_ref.dtype)


def shards(amplitudes, integrals, occ_irrep, tile_irrep):
    n_amp = lax.axis_size("amp")
    n_own = lax.axis_size("own")
    k_local, rows, width = amplitudes.shape
    n_tiles = tile_irrep.shape[0]
    slots = width * n_amp // TILE
    grain = gcd(width, TILE)
    wide = NI * slots * TILE
    depth = -(-k_local * width // LANES) * LANES
    vmem, hbm = (pl.BlockSpec(memory_space=m) for m in (pltpu.VMEM, pltpu.HBM))
    labeled = jax.ShapeDtypeStruct((LABELS, wide, depth), jnp.bfloat16)
    a, w = pl.pallas_call(
        functools.partial(pack_kernel, n_tiles, slots),
        out_shape=(labeled, labeled),
        in_specs=[hbm] * 4,
        out_specs=(vmem, vmem),
        scratch_shapes=[
            pltpu.VMEM((k_local, width, rows), jnp.bfloat16),
            pltpu.VMEM((LABELS, k_local, width // grain, grain, rows), jnp.bfloat16),
            pltpu.VMEM((rows, depth), jnp.bfloat16),
            pltpu.SMEM(occ_irrep.shape, jnp.int32),
            pltpu.SMEM(tile_irrep.shape, jnp.int32),
            pltpu.SMEM((LABELS * slots,), jnp.int32),
            pltpu.SMEM((LABELS,), jnp.int32),
            pltpu.SemaphoreType.DMA((3,)),
            pltpu.SemaphoreType.DMA((LABELS, k_local, width // grain)),
        ],
        compiler_params=pltpu.CompilerParams(vmem_limit_bytes=40 * 2**20),
        name="pack",
    )(*(pltpu.with_memory_space_constraint(x, pltpu.HBM) for x in (jnp.swapaxes(amplitudes, 1, 2), integrals, occ_irrep, tile_irrep)))

    share = rows // (n_amp * n_own)
    n_y, n_hi, n_lo = split_of(n_amp, n_own)
    n_flat = n_y * n_lo
    bufs = []
    for lanes, leads in (
        (wide - LANES, ((n_flat - 1, n_hi), (n_hi - 1,))),
        (LANES, ((n_hi - 1, n_flat), (n_flat - 1,))),
    ):
        for lead in leads:
            bufs += [pltpu.VMEM(lead + (share, lanes), jnp.int16)] * 2
            bufs += [pltpu.VMEM(lead + (1, lanes), jnp.float32)] * 2
            bufs += [pltpu.SemaphoreType.DMA((2, lead[0], 2))] * 2
    return pl.pallas_call(
        functools.partial(cycle_kernel, n_y, n_hi, n_lo, slots),
        out_shape=jax.ShapeDtypeStruct((share, rows), jnp.bfloat16),
        in_specs=[vmem, vmem, hbm, hbm],
        out_specs=vmem,
        scratch_shapes=[
            pltpu.VMEM((LABELS, slots, TILE, wide), jnp.float32),
            pltpu.VMEM((n_y, rows // n_y, wide) if share % 8 == 0 else (n_y, 2 * n_own, share, wide), jnp.float32),
            pltpu.VMEM((n_y, n_own, share, wide), jnp.int16),
            pltpu.VMEM((n_y, n_own, share, wide), jnp.int16),
            pltpu.VMEM((n_y, n_own, 1, wide), jnp.float32),
            pltpu.VMEM((n_y, n_own, 1, wide), jnp.float32),
            pltpu.VMEM((wide // LANES, share, LANES), jnp.float32),
            pltpu.SMEM(occ_irrep.shape, jnp.int32),
            pltpu.SMEM(tile_irrep.shape, jnp.int32),
            pltpu.SMEM((n_tiles,), jnp.int32),
            pltpu.SemaphoreType.DMA((2,)),
            pltpu.SemaphoreType.DMA((2, n_y)),
            pltpu.SemaphoreType.DMA((2, n_y)),
        ]
        + bufs,
        compiler_params=pltpu.CompilerParams(collective_id=0, has_side_effects=True, vmem_limit_bytes=40 * 2**20),
        name="cycle",
    )(a, w, *(pltpu.with_memory_space_constraint(x, pltpu.HBM) for x in (occ_irrep, tile_irrep)))


def solution(mesh):
    return jax.shard_map(
        shards,
        mesh=mesh,
        in_specs=(P("own", None, "amp"), P("own", None, None), P(), P()),
        out_specs=P(("amp", "own"), None),
        check_vma=False,
    )
```

```python
import functools

import jax
import jax.numpy as jnp
from jax import lax
from jax.experimental import pallas as pl
from jax.experimental.pallas import tpu as pltpu
from jax.sharding import PartitionSpec as P

TILE = 64
NI = 2
LABELS = 8
LANES = 128
LEVELS = 32767.0
LEAST = 1e-30
MESH = pl.DeviceIdType.MESH


def gcd(a, b):
    return a if b == 0 else gcd(b, a % b)


def pack_kernel(n_tiles, slots, n_amp, grain, amp_hbm, int_hbm, occ_hbm, tile_hbm, a_ref, w_ref, amp_ref, int_ref, turn_ref, occ_ref, tile_ref, tile_of, count, small_sems, sems):
    k_local, width, rows = amp_ref.shape
    depth = a_ref.shape[2]
    amp_index = lax.axis_index("amp")
    own_index = lax.axis_index("own")

    tile_copy = pltpu.make_async_copy(tile_hbm, tile_ref, small_sems.at[0])
    occ_copy = pltpu.make_async_copy(occ_hbm, occ_ref, small_sems.at[1])
    amp_copy = pltpu.make_async_copy(amp_hbm, amp_ref, small_sems.at[2])
    tile_copy.start()
    occ_copy.start()
    amp_copy.start()
    for i in range(LABELS):
        count[i] = 0
        for s in range(slots):
            tile_of[i * slots + s] = -1
    tile_copy.wait()
    for t in range(n_tiles):
        lab = tile_ref[t]
        rank = count[lab]
        tile_of[lab * slots + rank] = t
        count[lab] = rank + 1
    occ_copy.wait()
    k_lab = [occ_ref[NI + own_index * k_local + k] for k in range(k_local)]

    heads = sorted({min(width, TILE - at * width % TILE) for at in range(n_amp)})
    head_here = jnp.minimum(width, TILE - amp_index * width % TILE)

    def tile_at(lab, k, row):
        at = amp_index * width + row
        return tile_of[jnp.bitwise_xor(lab, k_lab[k]) * slots + at // TILE], at % TILE

    for head in heads:

        @pl.when(head_here == head)
        def _():
            def fetch(lab, carry):
                for k in range(k_local):
                    for row, size in ((0, head), (head, width - head)):
                        if size:
                            t, at = tile_at(lab, k, row)
                            start = pl.multiple_of(jnp.maximum(t, 0) * TILE + at, grain)
                            to = int_ref.at[lab, k, pl.ds(row, size), :]
                            pltpu.make_async_copy(int_hbm.at[k, pl.ds(start, size), :], to, sems.at[lab]).start()
                return carry

            lax.fori_loop(0, LABELS, fetch, 0)

    low = lax.broadcasted_iota(jnp.int32, (width, LANES), 1) < TILE
    row = lax.broadcasted_iota(jnp.int32, (width, LANES), 0)

    def turned(parts):
        spare = depth - k_local * width
        if spare:
            parts = parts + [jnp.zeros((spare, LANES), a_ref.dtype)]
        return jnp.concatenate(parts, axis=0).T

    amp_copy.wait()

    def turn(m, carry):
        at = pl.ds(pl.multiple_of(m * LANES, LANES), LANES)
        turn_ref[at, :] = turned([amp_ref[k, :, at] for k in range(k_local)])
        return carry

    lax.fori_loop(0, rows // LANES, turn, 0)

    def block(lab, carry):
        pltpu.make_async_copy(int_hbm.at[:, pl.ds(0, width), :], int_ref.at[lab], sems.at[lab]).wait()
        held = []
        for k in range(k_local):
            there = [jnp.where(tile_at(lab, k, at)[0] >= 0, 1, 0) for at in (0, width - 1)]
            held.append(jnp.where(row < head_here, there[0], there[1]) > 0)
        zero = jnp.zeros((width, LANES), w_ref.dtype)
        tiles = []
        for q in range(NI * slots):
            i, j = q // slots, q % slots
            tiles.append(i * n_tiles + jnp.maximum(tile_of[jnp.bitwise_xor(lab, occ_ref[i]) * slots + j], 0))
        for q, u in enumerate(tiles):
            a_ref[lab, q * TILE : (q + 1) * TILE, :] = turn_ref[pl.ds(pl.multiple_of(u * TILE, TILE), TILE), :]
        for q in range(0, NI * slots, 2):
            both = []
            for h in range(2):
                u = tiles[q + h]
                at = pl.ds(pl.multiple_of(u // 2 * LANES, LANES), LANES)
                both.append([pltpu.roll(int_ref[lab, k, :, at], (u + h) % 2 * TILE, 1) for k in range(k_local)])
            w_ref[lab, q * TILE : (q + 2) * TILE, :] = turned([jnp.where(here, jnp.where(low, *pair), zero) for here, *pair in zip(held, *both)])
        return carry

    lax.fori_loop(0, LABELS, block, 0)


def split_of(n_amp, n_own):
    lo = 2 if n_own <= 8 else 8
    return n_amp // 2, n_own // lo, lo


def cycle_kernel(n_y, n_hi, n_lo, slots, a_ref, w_ref, occ_hbm, tile_hbm, out_ref, s_ref, x_ref, near_q, near_got, near_m, near_got_m, fin_ref, occ_ref, tile_ref, rank_ref, small_sems, near_send, near_recv, *bufs):
    n_own = n_hi * n_lo
    share = fin_ref.shape[1]
    n_tiles = tile_ref.shape[0]
    half = slots * TILE
    wide = NI * half
    amp, own = lax.axis_index("amp"), lax.axis_index("own")
    y, core, hi, lo = amp // 2, amp % 2, own // n_lo, own % n_lo
    n_flat = n_y * n_lo
    split = wide - LANES
    parts = [(0, split), (split, wide)]
    cuts = [[(1, n_hi - 1), (0, 1)], [(n_lo, n_lo), (1, n_lo - 1), (0, 1)] if n_y == 2 else [(1, n_flat - 1), (0, 1)]]
    other = (y * 2 + 1 - core, own)

    def at_of(flat, high):
        return (y + flat // n_lo) % n_y, (hi + high) % n_hi, (lo + flat % n_lo) % n_lo

    def id_of(flat, high):
        y_at, hi_at, lo_at = at_of(flat, high)
        return (y_at * 2 + core, hi_at * n_lo + lo_at)

    tile_copy = pltpu.make_async_copy(tile_hbm, tile_ref, small_sems.at[0])
    occ_copy = pltpu.make_async_copy(occ_hbm, occ_ref, small_sems.at[1])
    tile_copy.start()
    occ_copy.start()
    barrier = pltpu.get_barrier_semaphore()
    pl.semaphore_signal(barrier, inc=1, device_id=other, device_id_type=MESH)
    for j in range(1, n_flat):
        back = (n_y - j // n_lo) % n_y * n_lo + (n_lo - j % n_lo) % n_lo
        pl.semaphore_signal(barrier, inc=1, device_id=id_of(back, 0), device_id_type=MESH)
    for j in range(1, n_hi):
        pl.semaphore_signal(barrier, inc=1, device_id=id_of(0, n_hi - j), device_id_type=MESH)

    def coded(x):
        most = jnp.maximum(jnp.max(jnp.abs(x), axis=0, keepdims=True), LEAST)
        return jnp.round(x * (LEVELS / most)).astype(jnp.int32).astype(jnp.int16), most * (1.0 / LEVELS)

    def plain(q, m):
        return q.astype(jnp.int32).astype(jnp.float32) * m

    def remote(src, dst, send, recv, to):
        return pltpu.make_async_remote_copy(src_ref=src, dst_ref=dst, send_sem=send, recv_sem=recv, device_id=to, device_id_type=MESH)

    def near(y_at):
        return [
            remote(src.at[y_at], dst.at[y_at], near_send.at[which, y_at], near_recv.at[which, y_at], other)
            for which, (src, dst) in enumerate(((near_m, near_got_m), (near_q, near_got)))
        ]

    def block(y_at, core_at, own_at, lanes):
        at = core_at * n_own + own_at
        if len(x_ref.shape) == 4:
            return x_ref[y_at, at, :, lanes]
        return x_ref[y_at, pl.ds(pl.multiple_of(at * share, 8), share), lanes]

    def multiply(i):
        rows = pl.ds(pl.multiple_of(i * half, TILE), half)
        over = (((1,), (1,)), ((), ()))

        def step(lab, carry):
            s = lax.dot_general(a_ref[lab, rows, :], w_ref[lab], over, preferred_element_type=jnp.float32)
            s = s + lax.dot_general(w_ref[lab, rows, :], a_ref[lab], over, preferred_element_type=jnp.float32)
            s_ref[lab] = s.reshape(s_ref.shape[1:])
            return carry

        lax.fori_loop(0, LABELS, step, 0)

    def spread(y_at, i):
        count = NI * n_tiles // n_y
        for n in range(count):
            t = y_at * count + n - i * n_tiles
            lab = jnp.bitwise_xor(occ_ref[i], tile_ref[t])
            rank = rank_ref[t]
            if len(x_ref.shape) == 3:
                x_ref[y_at, n * TILE : (n + 1) * TILE] = s_ref[lab, rank]
                continue
            tile = s_ref[lab, rank]
            for b in range(n * TILE // share, -(-(n + 1) * TILE // share)):
                low, high = max(n * TILE, b * share), min((n + 1) * TILE, (b + 1) * share)
                x_ref[y_at, b, low - b * share : high - b * share] = tile[low - n * TILE : high - n * TILE]

        def step(b, carry):
            near_q[y_at, b], near_m[y_at, b] = coded(block(y_at, 1 - core, b, slice(None)))
            return carry

        lax.fori_loop(0, n_own, step, 0)

    def pair(p, flat, high):
        y_at, hi_at, lo_at = at_of(flat, high)
        own_at = hi_at * n_lo + lo_at
        lanes = slice(*parts[p])
        return block(y_at, core, own_at, lanes) + plain(near_got[y_at, own_at, :, lanes], near_got_m[y_at, own_at, :, lanes])

    def far(p, s, j, cut):
        q_send, q_got, m_send, m_got, send, recv = bufs[12 * p + 6 * s :][:6]
        to = id_of(j, 0) if p == s else id_of(0, j)
        at = (j - 1,) if s else (j - 1, pl.ds(cuts[p][cut][0], cuts[p][cut][1]))
        return [
            remote(src.at[at], dst.at[at], send.at[which, j - 1, cut], recv.at[which, j - 1, cut], to)
            for which, (src, dst) in enumerate(((m_send, m_got), (q_send, q_got)))
        ]

    def first(p, cut, partners):
        q_send, _, m_send = bufs[12 * p :][:3]
        start, count = cuts[p][cut]
        for j in partners:
            for i in range(start, start + count):
                q_send[j - 1, i], m_send[j - 1, i] = coded(pair(0, j, i) if p == 0 else pair(1, i, j))
            for copy in far(p, 0, j, cut):
                copy.start()

    def total(p, i):
        _, q_got, _, m_got = bufs[12 * p :][:4]
        x = pair(p, 0, i) if p == 0 else pair(p, i, 0)
        for j in range(q_got.shape[0]):
            x = x + plain(q_got[j, i], m_got[j, i])
        return x

    def keep(p, x):
        for c in range((parts[p][1] - parts[p][0]) // LANES):
            fin_ref[parts[p][0] // LANES + c] = x[:, c * LANES : (c + 1) * LANES]

    def second(p, cut):
        q_send, _, m_send = bufs[12 * p + 6 :][:3]
        for j in range(cuts[p][cut][0], sum(cuts[p][cut])):
            q_send[j - 1], m_send[j - 1] = coded(total(p, j))
            for copy in far(p, 1, j, 0):
                copy.start()

    def last(p, x):
        _, q_got, _, m_got = bufs[12 * p + 6 :][:4]
        for j in range(q_got.shape[0]):
            x = x + plain(q_got[j], m_got[j])
        keep(p, x)

    if n_y == 2:
        stages = [([1], [(1 - y, 1 - y)]), ([0], [(y, y)])]
    else:
        stages = [(list(range(n_y)), [(y_at, y_at * NI // n_y) for y_at in range(n_y)])]

    done = None
    ready = False
    for _, work in stages:
        for y_at, i in work:
            if done is None or n_y == 2 or done != i:
                multiply(i)
                done = i
            if not ready:
                ready = True
                tile_copy.wait()
                occ_copy.wait()
                for t in range(n_tiles):
                    rank = jnp.int32(0)
                    for before in range(t):
                        rank = rank + jnp.where(tile_ref[before] == tile_ref[t], 1, 0)
                    rank_ref[t] = jnp.minimum(rank, slots - 1)
                spread(y_at, i)
                pl.semaphore_wait(barrier, n_flat + n_hi - 1)
            else:
                spread(y_at, i)
            for copy in near(y_at):
                copy.start()
    def received(p, s, cut):
        for j in range(1, n_flat if p == s else n_hi):
            for copy in far(p, s, j, cut):
                copy.wait_recv()

    def near_done(work):
        for y_at, _ in work:
            for copy in near(y_at):
                copy.wait_recv()

    near_done(stages[0][1])
    if n_y == 2:
        first(0, 0, range(n_lo, n_flat))
        first(1, 0, range(1, n_hi))
        near_done(stages[1][1])
        first(0, 0, range(1, n_lo))
        first(1, 1, range(1, n_hi))
    else:
        first(0, 0, range(1, n_flat))
        first(1, 0, range(1, n_hi))
    first(0, 1, range(1, n_flat))
    first(1, len(cuts[1]) - 1, range(1, n_hi))
    for p in range(2):
        for cut in range(len(cuts[p]) - 1):
            received(p, 0, cut)
            second(p, cut)
    kept = []
    for p in range(2):
        received(p, 0, len(cuts[p]) - 1)
        kept.append(total(p, 0))
    for p in range(2):
        received(p, 1, 0)
        last(p, kept[p])
    for _, work in stages:
        for y_at, _ in work:
            for copy in near(y_at):
                copy.wait_send()
    for p in range(2):
        for s in range(2):
            for cut in range(len(cuts[p]) if s == 0 else 1):
                for j in range(1, n_flat if p == s else n_hi):
                    for copy in far(p, s, j, cut):
                        copy.wait_send()
    expand((amp * n_own + own) * share, slots, fin_ref, occ_ref, tile_ref, rank_ref, out_ref)


def expand(base, slots, x_ref, occ_ref, tile_ref, rank_ref, out_ref):
    share = x_ref.shape[1]
    n_tiles = tile_ref.shape[0]
    count = NI * n_tiles
    labs = [jnp.bitwise_xor(occ_ref[u // n_tiles], tile_ref[u % n_tiles]) for u in range(count)]

    def label(u):
        return jnp.bitwise_xor(occ_ref[u // n_tiles], tile_ref[u % n_tiles])

    first = base // TILE
    row = base + lax.broadcasted_iota(jnp.int32, (share, LANES), 0)
    low = lax.broadcasted_iota(jnp.int32, (share, LANES), 1) < TILE
    row_lab = jnp.where(row < (first + 1) * TILE, label(first), label(jnp.minimum(first + 1, count - 1)))
    for u in range(0, count, 2):
        slot = [(u + h) // n_tiles * slots + rank_ref[(u + h) % n_tiles] for h in range(2)]
        turned = [pltpu.roll(x_ref[at // 2], (at + h) % 2 * TILE, 1) for h, at in enumerate(slot)]
        match = row_lab == jnp.where(low, labs[u], labs[u + 1])
        out_ref[:, u * TILE : (u + 2) * TILE] = jnp.where(match, jnp.where(low, *turned), 0.0).astype(out_ref.dtype)


def shards(amplitudes, integrals, occ_irrep, tile_irrep):
    n_amp = lax.axis_size("amp")
    n_own = lax.axis_size("own")
    k_local, rows, width = amplitudes.shape
    n_tiles = tile_irrep.shape[0]
    slots = width * n_amp // TILE
    grain = gcd(width, TILE)
    wide = NI * slots * TILE
    depth = -(-k_local * width // LANES) * LANES
    vmem, hbm = (pl.BlockSpec(memory_space=m) for m in (pltpu.VMEM, pltpu.HBM))
    labeled = jax.ShapeDtypeStruct((LABELS, wide, depth), jnp.bfloat16)
    a, w = pl.pallas_call(
        functools.partial(pack_kernel, n_tiles, slots, n_amp, grain),
        out_shape=(labeled, labeled),
        in_specs=[hbm] * 4,
        out_specs=(vmem, vmem),
        scratch_shapes=[
            pltpu.VMEM((k_local, width, rows), jnp.bfloat16),
            pltpu.VMEM((LABELS, k_local, width, rows), jnp.bfloat16),
            pltpu.VMEM((rows, depth), jnp.bfloat16),
            pltpu.SMEM(occ_irrep.shape, jnp.int32),
            pltpu.SMEM(tile_irrep.shape, jnp.int32),
            pltpu.SMEM((LABELS * slots,), jnp.int32),
            pltpu.SMEM((LABELS,), jnp.int32),
            pltpu.SemaphoreType.DMA((3,)),
            pltpu.SemaphoreType.DMA((LABELS,)),
        ],
        compiler_params=pltpu.CompilerParams(vmem_limit_bytes=40 * 2**20),
        name="pack",
    )(*(pltpu.with_memory_space_constraint(x, pltpu.HBM) for x in (jnp.swapaxes(amplitudes, 1, 2), integrals, occ_irrep, tile_irrep)))

    share = rows // (n_amp * n_own)
    n_y, n_hi, n_lo = split_of(n_amp, n_own)
    n_flat = n_y * n_lo
    bufs = []
    for lanes, leads in (
        (wide - LANES, ((n_flat - 1, n_hi), (n_hi - 1,))),
        (LANES, ((n_hi - 1, n_flat), (n_flat - 1,))),
    ):
        for lead in leads:
            bufs += [pltpu.VMEM(lead + (share, lanes), jnp.int16)] * 2
            bufs += [pltpu.VMEM(lead + (1, lanes), jnp.float32)] * 2
            bufs += [pltpu.SemaphoreType.DMA((2, lead[0], 3))] * 2
    return pl.pallas_call(
        functools.partial(cycle_kernel, n_y, n_hi, n_lo, slots),
        out_shape=jax.ShapeDtypeStruct((share, rows), jnp.bfloat16),
        in_specs=[vmem, vmem, hbm, hbm],
        out_specs=vmem,
        scratch_shapes=[
            pltpu.VMEM((LABELS, slots, TILE, wide), jnp.float32),
            pltpu.VMEM((n_y, rows // n_y, wide) if share % 8 == 0 else (n_y, 2 * n_own, share, wide), jnp.float32),
            pltpu.VMEM((n_y, n_own, share, wide), jnp.int16),
            pltpu.VMEM((n_y, n_own, share, wide), jnp.int16),
            pltpu.VMEM((n_y, n_own, 1, wide), jnp.float32),
            pltpu.VMEM((n_y, n_own, 1, wide), jnp.float32),
            pltpu.VMEM((wide // LANES, share, LANES), jnp.float32),
            pltpu.SMEM(occ_irrep.shape, jnp.int32),
            pltpu.SMEM(tile_irrep.shape, jnp.int32),
            pltpu.SMEM((n_tiles,), jnp.int32),
            pltpu.SemaphoreType.DMA((2,)),
            pltpu.SemaphoreType.DMA((2, n_y)),
            pltpu.SemaphoreType.DMA((2, n_y)),
        ]
        + bufs,
        compiler_params=pltpu.CompilerParams(collective_id=0, has_side_effects=True, vmem_limit_bytes=40 * 2**20),
        name="cycle",
    )(a, w, *(pltpu.with_memory_space_constraint(x, pltpu.HBM) for x in (occ_irrep, tile_irrep)))


def solution(mesh):
    return jax.shard_map(
        shards,
        mesh=mesh,
        in_specs=(P("own", None, "amp"), P("own", None, None), P(), P()),
        out_specs=P(("amp", "own"), None),
        check_vma=False,
    )
```

```python
import functools

import jax
import jax.numpy as jnp
from jax import lax
from jax.experimental import pallas as pl
from jax.experimental.pallas import tpu as pltpu
from jax.sharding import PartitionSpec as P

TILE = 64
NI = 2
LABELS = 8
LANES = 128
LEVELS = 32767.0
LEAST = 1e-30
MESH = pl.DeviceIdType.MESH


def gcd(a, b):
    return a if b == 0 else gcd(b, a % b)


def pack_kernel(n_tiles, slots, n_amp, grain, amp_hbm, int_hbm, occ_hbm, tile_hbm, a_ref, w_ref, amp_ref, int_ref, turn_ref, occ_ref, tile_ref, tile_of, count, small_sems, sems):
    k_local, width, rows = amp_ref.shape
    depth = a_ref.shape[2]
    amp_index = lax.axis_index("amp")
    own_index = lax.axis_index("own")

    tile_copy = pltpu.make_async_copy(tile_hbm, tile_ref, small_sems.at[0])
    occ_copy = pltpu.make_async_copy(occ_hbm, occ_ref, small_sems.at[1])
    amp_copy = pltpu.make_async_copy(amp_hbm, amp_ref, small_sems.at[2])
    tile_copy.start()
    occ_copy.start()
    amp_copy.start()
    for i in range(LABELS):
        count[i] = 0
        for s in range(slots):
            tile_of[i * slots + s] = -1
    tile_copy.wait()
    for t in range(n_tiles):
        lab = tile_ref[t]
        rank = count[lab]
        tile_of[lab * slots + rank] = t
        count[lab] = rank + 1
    occ_copy.wait()
    k_lab = [occ_ref[NI + own_index * k_local + k] for k in range(k_local)]

    heads = sorted({min(width, TILE - at * width % TILE) for at in range(n_amp)})
    head_here = jnp.minimum(width, TILE - amp_index * width % TILE)

    def tile_at(lab, k, row):
        at = amp_index * width + row
        return tile_of[jnp.bitwise_xor(lab, k_lab[k]) * slots + at // TILE], at % TILE

    for head in heads:

        @pl.when(head_here == head)
        def _():
            def fetch(lab, carry):
                for k in range(k_local):
                    for row, size in ((0, head), (head, width - head)):
                        if size:
                            t, at = tile_at(lab, k, row)
                            start = pl.multiple_of(jnp.where(t < 0, lab, t) * TILE + at, grain)
                            to = int_ref.at[lab, k, pl.ds(row, size), :]
                            pltpu.make_async_copy(int_hbm.at[k, pl.ds(start, size), :], to, sems.at[lab]).start()
                return carry

            lax.fori_loop(0, LABELS, fetch, 0)

    low = lax.broadcasted_iota(jnp.int32, (width, LANES), 1) < TILE
    row = lax.broadcasted_iota(jnp.int32, (width, LANES), 0)

    def turned(parts):
        spare = depth - k_local * width
        if spare:
            parts = parts + [jnp.zeros((spare, LANES), a_ref.dtype)]
        return jnp.concatenate(parts, axis=0).T

    amp_copy.wait()

    def turn(m, carry):
        at = pl.ds(pl.multiple_of(m * LANES, LANES), LANES)
        turn_ref[at, :] = turned([amp_ref[k, :, at] for k in range(k_local)])
        return carry

    lax.fori_loop(0, rows // LANES, turn, 0, unroll=3)

    def block(lab, carry):
        pltpu.make_async_copy(int_hbm.at[:, pl.ds(0, width), :], int_ref.at[lab], sems.at[lab]).wait()
        held = []
        for k in range(k_local):
            there = [jnp.where(tile_at(lab, k, at)[0] >= 0, 1, 0) for at in (0, width - 1)]
            held.append(jnp.where(row < head_here, there[0], there[1]) > 0)
        zero = jnp.zeros((width, LANES), w_ref.dtype)
        tiles = []
        for q in range(NI * slots):
            i, j = q // slots, q % slots
            tiles.append(i * n_tiles + jnp.maximum(tile_of[jnp.bitwise_xor(lab, occ_ref[i]) * slots + j], 0))
        for q, u in enumerate(tiles):
            a_ref[lab, q * TILE : (q + 1) * TILE, :] = turn_ref[pl.ds(pl.multiple_of(u * TILE, TILE), TILE), :]
        for q in range(0, NI * slots, 2):
            both = []
            for h in range(2):
                u = tiles[q + h]
                at = pl.ds(pl.multiple_of(u // 2 * LANES, LANES), LANES)
                both.append([pltpu.roll(int_ref[lab, k, :, at], (u + h) % 2 * TILE, 1) for k in range(k_local)])
            w_ref[lab, q * TILE : (q + 2) * TILE, :] = turned([jnp.where(here, jnp.where(low, *pair), zero) for here, *pair in zip(held, *both)])
        return carry

    lax.fori_loop(0, LABELS, block, 0)


def split_of(n_amp, n_own):
    lo = 2 if n_own <= 8 else 8
    return n_amp // 2, n_own // lo, lo


def cycle_kernel(n_y, n_hi, n_lo, slots, a_ref, w_ref, occ_hbm, tile_hbm, out_ref, s_ref, x_ref, near_q, near_got, near_m, near_got_m, fin_ref, both_ref, occ_ref, tile_ref, rank_ref, small_sems, near_send, near_recv, *bufs):
    n_own = n_hi * n_lo
    share = fin_ref.shape[1]
    n_tiles = tile_ref.shape[0]
    half = slots * TILE
    wide = NI * half
    amp, own = lax.axis_index("amp"), lax.axis_index("own")
    y, core, hi, lo = amp // 2, amp % 2, own // n_lo, own % n_lo
    n_flat = n_y * n_lo
    split = wide - LANES
    parts = [(0, split), (split, wide)]
    cuts = [[(1, n_hi - 1), (0, 1)], [(n_lo, n_lo), (1, n_lo - 1), (0, 1)] if n_y == 2 else [(1, n_flat - 1), (0, 1)]]
    other = (y * 2 + 1 - core, own)

    def at_of(flat, high):
        return (y + flat // n_lo) % n_y, (hi + high) % n_hi, (lo + flat % n_lo) % n_lo

    def id_of(flat, high):
        y_at, hi_at, lo_at = at_of(flat, high)
        return (y_at * 2 + core, hi_at * n_lo + lo_at)

    tile_copy = pltpu.make_async_copy(tile_hbm, tile_ref, small_sems.at[0])
    occ_copy = pltpu.make_async_copy(occ_hbm, occ_ref, small_sems.at[1])
    tile_copy.start()
    occ_copy.start()
    barrier = pltpu.get_barrier_semaphore()
    pl.semaphore_signal(barrier, inc=1, device_id=other, device_id_type=MESH)
    for j in range(1, n_flat):
        back = (n_y - j // n_lo) % n_y * n_lo + (n_lo - j % n_lo) % n_lo
        pl.semaphore_signal(barrier, inc=1, device_id=id_of(back, 0), device_id_type=MESH)
    for j in range(1, n_hi):
        pl.semaphore_signal(barrier, inc=1, device_id=id_of(0, n_hi - j), device_id_type=MESH)

    def coded(x):
        most = jnp.maximum(jnp.max(jnp.abs(x), axis=0, keepdims=True), LEAST)
        return jnp.round(x * (LEVELS / most)).astype(jnp.int32).astype(jnp.int16), most * (1.0 / LEVELS)

    def plain(q, m):
        return q.astype(jnp.int32).astype(jnp.float32) * m

    def remote(src, dst, send, recv, to):
        return pltpu.make_async_remote_copy(src_ref=src, dst_ref=dst, send_sem=send, recv_sem=recv, device_id=to, device_id_type=MESH)

    def near(y_at):
        return [
            remote(src.at[y_at], dst.at[y_at], near_send.at[which, y_at], near_recv.at[which, y_at], other)
            for which, (src, dst) in enumerate(((near_m, near_got_m), (near_q, near_got)))
        ]

    def block(y_at, core_at, own_at, lanes):
        at = core_at * n_own + own_at
        if len(x_ref.shape) == 4:
            return x_ref[y_at, at, :, lanes]
        return x_ref[y_at, pl.ds(pl.multiple_of(at * share, 8), share), lanes]

    def multiply(i):
        rows = pl.ds(pl.multiple_of(i * half, TILE), half)
        over = (((1,), (1,)), ((), ()))

        def step(lab, carry):
            s = lax.dot_general(a_ref[lab, rows, :], w_ref[lab], over, preferred_element_type=jnp.float32)
            s = s + lax.dot_general(w_ref[lab, rows, :], a_ref[lab], over, preferred_element_type=jnp.float32)
            s_ref[lab] = s.reshape(s_ref.shape[1:])
            return carry

        lax.fori_loop(0, LABELS, step, 0, unroll=4)

    def spread(y_at, i):
        count = NI * n_tiles // n_y
        for n in range(count):
            t = y_at * count + n - i * n_tiles
            lab = jnp.bitwise_xor(occ_ref[i], tile_ref[t])
            rank = rank_ref[t]
            if len(x_ref.shape) == 3:
                x_ref[y_at, n * TILE : (n + 1) * TILE] = s_ref[lab, rank]
                continue
            tile = s_ref[lab, rank]
            for b in range(n * TILE // share, -(-(n + 1) * TILE // share)):
                low, high = max(n * TILE, b * share), min((n + 1) * TILE, (b + 1) * share)
                x_ref[y_at, b, low - b * share : high - b * share] = tile[low - n * TILE : high - n * TILE]

        def step(b, carry):
            near_q[y_at, b], near_m[y_at, b] = coded(block(y_at, 1 - core, b, slice(None)))
            return carry

        lax.fori_loop(0, n_own, step, 0, unroll=4)

    def pair(p, flat, high):
        y_at, hi_at, lo_at = at_of(flat, high)
        own_at = hi_at * n_lo + lo_at
        lanes = slice(*parts[p])
        return block(y_at, core, own_at, lanes) + plain(near_got[y_at, own_at, :, lanes], near_got_m[y_at, own_at, :, lanes])

    def far(p, s, j, cut):
        q_send, q_got, m_send, m_got, send, recv = bufs[12 * p + 6 * s :][:6]
        to = id_of(j, 0) if p == s else id_of(0, j)
        at = (j - 1,) if s else (j - 1, pl.ds(cuts[p][cut][0], cuts[p][cut][1]))
        return [
            remote(src.at[at], dst.at[at], send.at[which, j - 1, cut], recv.at[which, j - 1, cut], to)
            for which, (src, dst) in enumerate(((m_send, m_got), (q_send, q_got)))
        ]

    def first(p, cut, partners):
        q_send, _, m_send = bufs[12 * p :][:3]
        start, count = cuts[p][cut]
        for j in partners:
            for i in range(start, start + count):
                q_send[j - 1, i], m_send[j - 1, i] = coded(pair(0, j, i) if p == 0 else pair(1, i, j))
            for copy in far(p, 0, j, cut):
                copy.start()

    def total(p, i):
        _, q_got, _, m_got = bufs[12 * p :][:4]
        x = pair(p, 0, i) if p == 0 else pair(p, i, 0)
        for j in range(q_got.shape[0]):
            x = x + plain(q_got[j, i], m_got[j, i])
        return x

    def keep(p, x):
        for c in range((parts[p][1] - parts[p][0]) // LANES):
            fin_ref[parts[p][0] // LANES + c] = x[:, c * LANES : (c + 1) * LANES]

    def second(p, cut):
        q_send, _, m_send = bufs[12 * p + 6 :][:3]
        for j in range(cuts[p][cut][0], sum(cuts[p][cut])):
            q_send[j - 1], m_send[j - 1] = coded(total(p, j))
            for copy in far(p, 1, j, 0):
                copy.start()

    def last(p, x):
        _, q_got, _, m_got = bufs[12 * p + 6 :][:4]
        for j in range(q_got.shape[0]):
            x = x + plain(q_got[j], m_got[j])
        keep(p, x)

    if n_y == 2:
        stages = [([1], [(1 - y, 1 - y)]), ([0], [(y, y)])]
    else:
        stages = [(list(range(n_y)), [(y_at, y_at * NI // n_y) for y_at in range(n_y)])]

    done = None
    ready = False
    for _, work in stages:
        for y_at, i in work:
            if done is None or n_y == 2 or done != i:
                multiply(i)
                done = i
            if not ready:
                ready = True
                tile_copy.wait()
                occ_copy.wait()
                for t in range(n_tiles):
                    rank = jnp.int32(0)
                    for before in range(t):
                        rank = rank + jnp.where(tile_ref[before] == tile_ref[t], 1, 0)
                    rank_ref[t] = jnp.minimum(rank, slots - 1)
                spread(y_at, i)
                pl.semaphore_wait(barrier, n_flat + n_hi - 1)
            else:
                spread(y_at, i)
            for copy in near(y_at):
                copy.start()
    def received(p, s, cut):
        for j in range(1, n_flat if p == s else n_hi):
            for copy in far(p, s, j, cut):
                copy.wait_recv()

    def near_done(work):
        for y_at, _ in work:
            for copy in near(y_at):
                copy.wait_recv()

    near_done(stages[0][1])
    if n_y == 2:
        first(0, 0, range(n_lo, n_flat))
        first(1, 0, range(1, n_hi))
        near_done(stages[1][1])
        first(0, 0, range(1, n_lo))
        first(1, 1, range(1, n_hi))
    else:
        first(0, 0, range(1, n_flat))
        first(1, 0, range(1, n_hi))
    first(0, 1, range(1, n_flat))
    first(1, len(cuts[1]) - 1, range(1, n_hi))
    for p in range(2):
        for cut in range(len(cuts[p]) - 1):
            received(p, 0, cut)
            second(p, cut)
    kept = []
    for p in range(2):
        received(p, 0, len(cuts[p]) - 1)
        kept.append(total(p, 0))
    for p in range(2):
        received(p, 1, 0)
        last(p, kept[p])
    for _, work in stages:
        for y_at, _ in work:
            for copy in near(y_at):
                copy.wait_send()
    for p in range(2):
        for s in range(2):
            for cut in range(len(cuts[p]) if s == 0 else 1):
                for j in range(1, n_flat if p == s else n_hi):
                    for copy in far(p, s, j, cut):
                        copy.wait_send()
    expand((amp * n_own + own) * share, slots, fin_ref, both_ref, occ_ref, tile_ref, rank_ref, out_ref)


def expand(base, slots, x_ref, both_ref, occ_ref, tile_ref, rank_ref, out_ref):
    share = x_ref.shape[1]
    n_tiles = tile_ref.shape[0]
    count = NI * n_tiles
    labs = [jnp.bitwise_xor(occ_ref[u // n_tiles], tile_ref[u % n_tiles]) for u in range(count)]

    def label(u):
        return jnp.bitwise_xor(occ_ref[u // n_tiles], tile_ref[u % n_tiles])

    first = base // TILE
    row = base + lax.broadcasted_iota(jnp.int32, (share, LANES), 0)
    low = lax.broadcasted_iota(jnp.int32, (share, LANES), 1) < TILE
    row_lab = jnp.where(row < (first + 1) * TILE, label(first), label(jnp.minimum(first + 1, count - 1)))
    for c in range(x_ref.shape[0]):
        both_ref[0, c] = x_ref[c]
        both_ref[1, c] = pltpu.roll(x_ref[c], TILE, 1)
    for u in range(0, count, 2):
        slot = [(u + h) // n_tiles * slots + rank_ref[(u + h) % n_tiles] for h in range(2)]
        turned = [both_ref[(at + h) % 2, at // 2] for h, at in enumerate(slot)]
        match = row_lab == jnp.where(low, labs[u], labs[u + 1])
        out_ref[:, u * TILE : (u + 2) * TILE] = jnp.where(match, jnp.where(low, *turned), 0.0).astype(out_ref.dtype)


def shards(amplitudes, integrals, occ_irrep, tile_irrep):
    n_amp = lax.axis_size("amp")
    n_own = lax.axis_size("own")
    k_local, rows, width = amplitudes.shape
    n_tiles = tile_irrep.shape[0]
    slots = width * n_amp // TILE
    grain = gcd(width, TILE)
    wide = NI * slots * TILE
    depth = -(-k_local * width // LANES) * LANES
    vmem, hbm = (pl.BlockSpec(memory_space=m) for m in (pltpu.VMEM, pltpu.HBM))
    labeled = jax.ShapeDtypeStruct((LABELS, wide, depth), jnp.bfloat16)
    a, w = pl.pallas_call(
        functools.partial(pack_kernel, n_tiles, slots, n_amp, grain),
        out_shape=(labeled, labeled),
        in_specs=[hbm] * 4,
        out_specs=(vmem, vmem),
        scratch_shapes=[
            pltpu.VMEM((k_local, width, rows), jnp.bfloat16),
            pltpu.VMEM((LABELS, k_local, width, rows), jnp.bfloat16),
            pltpu.VMEM((rows, depth), jnp.bfloat16),
            pltpu.SMEM(occ_irrep.shape, jnp.int32),
            pltpu.SMEM(tile_irrep.shape, jnp.int32),
            pltpu.SMEM((LABELS * slots,), jnp.int32),
            pltpu.SMEM((LABELS,), jnp.int32),
            pltpu.SemaphoreType.DMA((3,)),
            pltpu.SemaphoreType.DMA((LABELS,)),
        ],
        compiler_params=pltpu.CompilerParams(vmem_limit_bytes=40 * 2**20),
        name="pack",
    )(*(pltpu.with_memory_space_constraint(x, pltpu.HBM) for x in (jnp.swapaxes(amplitudes, 1, 2), integrals, occ_irrep, tile_irrep)))

    share = rows // (n_amp * n_own)
    n_y, n_hi, n_lo = split_of(n_amp, n_own)
    n_flat = n_y * n_lo
    bufs = []
    for lanes, leads in (
        (wide - LANES, ((n_flat - 1, n_hi), (n_hi - 1,))),
        (LANES, ((n_hi - 1, n_flat), (n_flat - 1,))),
    ):
        for lead in leads:
            bufs += [pltpu.VMEM(lead + (share, lanes), jnp.int16)] * 2
            bufs += [pltpu.VMEM(lead + (1, lanes), jnp.float32)] * 2
            bufs += [pltpu.SemaphoreType.DMA((2, lead[0], 3))] * 2
    return pl.pallas_call(
        functools.partial(cycle_kernel, n_y, n_hi, n_lo, slots),
        out_shape=jax.ShapeDtypeStruct((share, rows), jnp.bfloat16),
        in_specs=[vmem, vmem, hbm, hbm],
        out_specs=vmem,
        scratch_shapes=[
            pltpu.VMEM((LABELS, slots, TILE, wide), jnp.float32),
            pltpu.VMEM((n_y, rows // n_y, wide) if share % 8 == 0 else (n_y, 2 * n_own, share, wide), jnp.float32),
            pltpu.VMEM((n_y, n_own, share, wide), jnp.int16),
            pltpu.VMEM((n_y, n_own, share, wide), jnp.int16),
            pltpu.VMEM((n_y, n_own, 1, wide), jnp.float32),
            pltpu.VMEM((n_y, n_own, 1, wide), jnp.float32),
            pltpu.VMEM((wide // LANES, share, LANES), jnp.float32),
            pltpu.VMEM((2, wide // LANES, share, LANES), jnp.float32),
            pltpu.SMEM(occ_irrep.shape, jnp.int32),
            pltpu.SMEM(tile_irrep.shape, jnp.int32),
            pltpu.SMEM((n_tiles,), jnp.int32),
            pltpu.SemaphoreType.DMA((2,)),
            pltpu.SemaphoreType.DMA((2, n_y)),
            pltpu.SemaphoreType.DMA((2, n_y)),
        ]
        + bufs,
        compiler_params=pltpu.CompilerParams(collective_id=0, has_side_effects=True, vmem_limit_bytes=40 * 2**20),
        name="cycle",
    )(a, w, *(pltpu.with_memory_space_constraint(x, pltpu.HBM) for x in (occ_irrep, tile_irrep)))


def solution(mesh):
    return jax.shard_map(
        shards,
        mesh=mesh,
        in_specs=(P("own", None, "amp"), P("own", None, None), P(), P()),
        out_specs=P(("amp", "own"), None),
        check_vma=False,
    )
```

```python
import functools

import jax
import jax.numpy as jnp
from jax import lax
from jax.experimental import pallas as pl
from jax.experimental.pallas import tpu as pltpu
from jax.sharding import PartitionSpec as P

TILE = 64
NI = 2
LABELS = 8
LANES = 128
LEVELS = 32767.0
LEAST = 1e-30
MESH = pl.DeviceIdType.MESH


def gcd(a, b):
    return a if b == 0 else gcd(b, a % b)


def pack_kernel(n_tiles, slots, n_amp, grain, amp_hbm, int_hbm, occ_hbm, tile_hbm, a_ref, w_ref, amp_ref, int_ref, turn_ref, occ_ref, tile_ref, tile_of, count, small_sems, sems):
    k_local, width, rows = amp_ref.shape
    depth = a_ref.shape[2]
    amp_index = lax.axis_index("amp")
    own_index = lax.axis_index("own")

    tile_copy = pltpu.make_async_copy(tile_hbm, tile_ref, small_sems.at[0])
    occ_copy = pltpu.make_async_copy(occ_hbm, occ_ref, small_sems.at[1])
    amp_copy = pltpu.make_async_copy(amp_hbm, amp_ref, small_sems.at[2])
    tile_copy.start()
    occ_copy.start()
    amp_copy.start()
    for i in range(LABELS):
        count[i] = 0
        for s in range(slots):
            tile_of[i * slots + s] = -1
    tile_copy.wait()
    for t in range(n_tiles):
        lab = tile_ref[t]
        rank = count[lab]
        tile_of[lab * slots + rank] = t
        count[lab] = rank + 1
    occ_copy.wait()
    k_lab = [occ_ref[NI + own_index * k_local + k] for k in range(k_local)]

    heads = sorted({min(width, TILE - at * width % TILE) for at in range(n_amp)})
    head_here = jnp.minimum(width, TILE - amp_index * width % TILE)

    def tile_at(lab, k, row):
        at = amp_index * width + row
        return tile_of[jnp.bitwise_xor(lab, k_lab[k]) * slots + at // TILE], at % TILE

    for head in heads:

        @pl.when(head_here == head)
        def _():
            def fetch(lab, carry):
                for k in range(k_local):
                    for row, size in ((0, head), (head, width - head)):
                        if size:
                            t, at = tile_at(lab, k, row)
                            start = pl.multiple_of(jnp.where(t < 0, lab, t) * TILE + at, grain)
                            to = int_ref.at[lab, k, pl.ds(row, size), :]
                            pltpu.make_async_copy(int_hbm.at[k, pl.ds(start, size), :], to, sems.at[lab]).start()
                return carry

            lax.fori_loop(0, LABELS, fetch, 0)

    low = lax.broadcasted_iota(jnp.int32, (width, LANES), 1) < TILE
    row = lax.broadcasted_iota(jnp.int32, (width, LANES), 0)

    def turned(parts):
        spare = depth - k_local * width
        if spare:
            parts = parts + [jnp.zeros((spare, LANES), a_ref.dtype)]
        return jnp.concatenate(parts, axis=0).T

    amp_copy.wait()

    def turn(m, carry):
        at = pl.ds(pl.multiple_of(m * LANES, LANES), LANES)
        turn_ref[at, :] = turned([amp_ref[k, :, at] for k in range(k_local)])
        return carry

    lax.fori_loop(0, rows // LANES, turn, 0, unroll=3)

    def block(lab, carry):
        pltpu.make_async_copy(int_hbm.at[:, pl.ds(0, width), :], int_ref.at[lab], sems.at[lab]).wait()
        held = []
        for k in range(k_local):
            there = [jnp.where(tile_at(lab, k, at)[0] >= 0, 1, 0) for at in (0, width - 1)]
            held.append(jnp.where(row < head_here, there[0], there[1]) > 0)
        zero = jnp.zeros((width, LANES), w_ref.dtype)
        tiles = []
        for q in range(NI * slots):
            i, j = q // slots, q % slots
            tiles.append(i * n_tiles + jnp.maximum(tile_of[jnp.bitwise_xor(lab, occ_ref[i]) * slots + j], 0))
        for q, u in enumerate(tiles):
            a_ref[lab, q * TILE : (q + 1) * TILE, :] = turn_ref[pl.ds(pl.multiple_of(u * TILE, TILE), TILE), :]
        for q in range(0, NI * slots, 2):
            both = []
            for h in range(2):
                u = tiles[q + h]
                at = pl.ds(pl.multiple_of(u // 2 * LANES, LANES), LANES)
                both.append([pltpu.roll(int_ref[lab, k, :, at], (u + h) % 2 * TILE, 1) for k in range(k_local)])
            w_ref[lab, q * TILE : (q + 2) * TILE, :] = turned([jnp.where(here, jnp.where(low, *pair), zero) for here, *pair in zip(held, *both)])
        return carry

    lax.fori_loop(0, LABELS, block, 0)


def split_of(n_amp, n_own):
    lo = 2 if n_own <= 8 else 8
    return n_amp // 2, n_own // lo, lo


def cycle_kernel(n_y, n_hi, n_lo, slots, a_ref, w_ref, occ_hbm, tile_hbm, out_ref, s_ref, x_ref, near_q, near_got, near_m, near_got_m, fin_ref, both_ref, occ_ref, tile_ref, rank_ref, small_sems, near_send, near_recv, *bufs):
    n_own = n_hi * n_lo
    share = fin_ref.shape[1]
    n_tiles = tile_ref.shape[0]
    half = slots * TILE
    wide = NI * half
    amp, own = lax.axis_index("amp"), lax.axis_index("own")
    y, core, hi, lo = amp // 2, amp % 2, own // n_lo, own % n_lo
    n_flat = n_y * n_lo
    split = wide - LANES
    parts = [(0, split), (split, wide)]
    cuts = [[(1, n_hi - 1), (0, 1)], [(n_lo, n_lo), (1, n_lo - 1), (0, 1)] if n_y == 2 else [(1, n_flat - 1), (0, 1)]]
    other = (y * 2 + 1 - core, own)

    def at_of(flat, high):
        return (y + flat // n_lo) % n_y, (hi + high) % n_hi, (lo + flat % n_lo) % n_lo

    def id_of(flat, high):
        y_at, hi_at, lo_at = at_of(flat, high)
        return (y_at * 2 + core, hi_at * n_lo + lo_at)

    tile_copy = pltpu.make_async_copy(tile_hbm, tile_ref, small_sems.at[0])
    occ_copy = pltpu.make_async_copy(occ_hbm, occ_ref, small_sems.at[1])
    tile_copy.start()
    occ_copy.start()
    barrier = pltpu.get_barrier_semaphore()
    pl.semaphore_signal(barrier, inc=1, device_id=other, device_id_type=MESH)
    for j in range(1, n_flat):
        back = (n_y - j // n_lo) % n_y * n_lo + (n_lo - j % n_lo) % n_lo
        pl.semaphore_signal(barrier, inc=1, device_id=id_of(back, 0), device_id_type=MESH)
    for j in range(1, n_hi):
        pl.semaphore_signal(barrier, inc=1, device_id=id_of(0, n_hi - j), device_id_type=MESH)

    def coded(x):
        most = jnp.maximum(jnp.max(jnp.abs(x), axis=0, keepdims=True), LEAST)
        return jnp.round(x * (LEVELS / most)).astype(jnp.int32).astype(jnp.int16), most * (1.0 / LEVELS)

    def plain(q, m):
        return q.astype(jnp.int32).astype(jnp.float32) * m

    def remote(src, dst, send, recv, to):
        return pltpu.make_async_remote_copy(src_ref=src, dst_ref=dst, send_sem=send, recv_sem=recv, device_id=to, device_id_type=MESH)

    def near(y_at):
        return [
            remote(src.at[y_at], dst.at[y_at], near_send.at[which, y_at], near_recv.at[which, y_at], other)
            for which, (src, dst) in enumerate(((near_m, near_got_m), (near_q, near_got)))
        ]

    def block(y_at, core_at, own_at, lanes):
        at = core_at * n_own + own_at
        if len(x_ref.shape) == 4:
            return x_ref[y_at, at, :, lanes]
        return x_ref[y_at, pl.ds(pl.multiple_of(at * share, 8), share), lanes]

    def multiply(i):
        rows = pl.ds(pl.multiple_of(i * half, TILE), half)
        over = (((1,), (1,)), ((), ()))

        def step(lab, carry):
            s = lax.dot_general(a_ref[lab, rows, :], w_ref[lab], over, preferred_element_type=jnp.float32)
            s = s + lax.dot_general(w_ref[lab, rows, :], a_ref[lab], over, preferred_element_type=jnp.float32)
            s_ref[lab] = s.reshape(s_ref.shape[1:])
            return carry

        lax.fori_loop(0, LABELS, step, 0, unroll=4)

    def spread(y_at, i):
        count = NI * n_tiles // n_y
        for n in range(count):
            t = y_at * count + n - i * n_tiles
            lab = jnp.bitwise_xor(occ_ref[i], tile_ref[t])
            rank = rank_ref[t]
            if len(x_ref.shape) == 3:
                x_ref[y_at, n * TILE : (n + 1) * TILE] = s_ref[lab, rank]
                continue
            tile = s_ref[lab, rank]
            for b in range(n * TILE // share, -(-(n + 1) * TILE // share)):
                low, high = max(n * TILE, b * share), min((n + 1) * TILE, (b + 1) * share)
                x_ref[y_at, b, low - b * share : high - b * share] = tile[low - n * TILE : high - n * TILE]

        def step(b, carry):
            near_q[y_at, b], near_m[y_at, b] = coded(block(y_at, 1 - core, b, slice(None)))
            return carry

        lax.fori_loop(0, n_own, step, 0, unroll=4)

    def pair(p, flat, high):
        y_at, hi_at, lo_at = at_of(flat, high)
        own_at = hi_at * n_lo + lo_at
        lanes = slice(*parts[p])
        return block(y_at, core, own_at, lanes) + plain(near_got[y_at, own_at, :, lanes], near_got_m[y_at, own_at, :, lanes])

    def far(p, s, j, cut):
        q_send, q_got, m_send, m_got, send, recv = bufs[12 * p + 6 * s :][:6]
        to = id_of(j, 0) if p == s else id_of(0, j)
        at = (j - 1,) if s else (j - 1, pl.ds(cuts[p][cut][0], cuts[p][cut][1]))
        return [
            remote(src.at[at], dst.at[at], send.at[which, j - 1, cut], recv.at[which, j - 1, cut], to)
            for which, (src, dst) in enumerate(((m_send, m_got), (q_send, q_got)))
        ]

    def first(p, cut, partners):
        q_send, _, m_send = bufs[12 * p :][:3]
        start, count = cuts[p][cut]
        for j in partners:
            for i in range(start, start + count):
                q_send[j - 1, i], m_send[j - 1, i] = coded(pair(0, j, i) if p == 0 else pair(1, i, j))
            for copy in far(p, 0, j, cut):
                copy.start()

    def total(p, i):
        _, q_got, _, m_got = bufs[12 * p :][:4]
        x = pair(p, 0, i) if p == 0 else pair(p, i, 0)
        for j in range(q_got.shape[0]):
            x = x + plain(q_got[j, i], m_got[j, i])
        return x

    def keep(p, x):
        for c in range((parts[p][1] - parts[p][0]) // LANES):
            fin_ref[parts[p][0] // LANES + c] = x[:, c * LANES : (c + 1) * LANES]

    def second(p, cut):
        q_send, _, m_send = bufs[12 * p + 6 :][:3]
        for j in range(cuts[p][cut][0], sum(cuts[p][cut])):
            q_send[j - 1], m_send[j - 1] = coded(total(p, j))
            for copy in far(p, 1, j, 0):
                copy.start()

    def last(p, x):
        _, q_got, _, m_got = bufs[12 * p + 6 :][:4]
        for j in range(q_got.shape[0]):
            x = x + plain(q_got[j], m_got[j])
        keep(p, x)

    if n_y == 2:
        stages = [([1], [(1 - y, 1 - y)]), ([0], [(y, y)])]
    else:
        stages = [(list(range(n_y)), [(y_at, y_at * NI // n_y) for y_at in range(n_y)])]

    done = None
    ready = False
    for _, work in stages:
        for y_at, i in work:
            if done is None or n_y == 2 or done != i:
                multiply(i)
                done = i
            if not ready:
                ready = True
                tile_copy.wait()
                occ_copy.wait()
                for t in range(n_tiles):
                    rank = jnp.int32(0)
                    for before in range(t):
                        rank = rank + jnp.where(tile_ref[before] == tile_ref[t], 1, 0)
                    rank_ref[t] = jnp.minimum(rank, slots - 1)
                spread(y_at, i)
                pl.semaphore_wait(barrier, n_flat + n_hi - 1)
            else:
                spread(y_at, i)
            for copy in near(y_at):
                copy.start()
    def received(p, s, cut):
        for j in range(1, n_flat if p == s else n_hi):
            for copy in far(p, s, j, cut):
                copy.wait_recv()

    def left(p, s, cut):
        for j in range(1, n_flat if p == s else n_hi):
            for copy in far(p, s, j, cut):
                copy.wait_send()

    def near_done(work):
        for y_at, _ in work:
            for copy in near(y_at):
                copy.wait_recv()

    near_done(stages[0][1])
    if n_y == 2:
        first(0, 0, range(n_flat - 1, n_lo - 1, -1))
        first(1, 0, range(1, n_hi))
        near_done(stages[1][1])
        first(0, 0, range(1, n_lo))
        first(1, 1, range(1, n_hi))
    else:
        first(0, 0, range(1, n_flat))
        first(1, 0, range(1, n_hi))
    first(0, 1, range(1, n_flat))
    first(1, len(cuts[1]) - 1, range(1, n_hi))
    for p in range(2):
        for cut in range(len(cuts[p]) - 1):
            received(p, 0, cut)
            second(p, cut)
    kept = []
    for p in range(2):
        received(p, 0, len(cuts[p]) - 1)
        kept.append(total(p, 0))
    for _, work in stages:
        for y_at, _ in work:
            for copy in near(y_at):
                copy.wait_send()
    for p in range(2):
        for cut in range(len(cuts[p])):
            left(p, 0, cut)
    for p in range(2):
        left(p, 1, 0)
    for p in range(2):
        received(p, 1, 0)
        last(p, kept[p])
    expand((amp * n_own + own) * share, slots, fin_ref, both_ref, occ_ref, tile_ref, rank_ref, out_ref)


def expand(base, slots, x_ref, both_ref, occ_ref, tile_ref, rank_ref, out_ref):
    share = x_ref.shape[1]
    n_tiles = tile_ref.shape[0]
    count = NI * n_tiles
    labs = [jnp.bitwise_xor(occ_ref[u // n_tiles], tile_ref[u % n_tiles]) for u in range(count)]

    def label(u):
        return jnp.bitwise_xor(occ_ref[u // n_tiles], tile_ref[u % n_tiles])

    first = base // TILE
    row = base + lax.broadcasted_iota(jnp.int32, (share, LANES), 0)
    low = lax.broadcasted_iota(jnp.int32, (share, LANES), 1) < TILE
    row_lab = jnp.where(row < (first + 1) * TILE, label(first), label(jnp.minimum(first + 1, count - 1)))
    for c in range(x_ref.shape[0]):
        both_ref[0, c] = x_ref[c]
        both_ref[1, c] = pltpu.roll(x_ref[c], TILE, 1)
    for u in range(0, count, 2):
        slot = [(u + h) // n_tiles * slots + rank_ref[(u + h) % n_tiles] for h in range(2)]
        turned = [both_ref[(at + h) % 2, at // 2] for h, at in enumerate(slot)]
        match = row_lab == jnp.where(low, labs[u], labs[u + 1])
        out_ref[:, u * TILE : (u + 2) * TILE] = jnp.where(match, jnp.where(low, *turned), 0.0).astype(out_ref.dtype)


def shards(amplitudes, integrals, occ_irrep, tile_irrep):
    n_amp = lax.axis_size("amp")
    n_own = lax.axis_size("own")
    k_local, rows, width = amplitudes.shape
    n_tiles = tile_irrep.shape[0]
    slots = width * n_amp // TILE
    grain = gcd(width, TILE)
    wide = NI * slots * TILE
    depth = -(-k_local * width // LANES) * LANES
    vmem, hbm = (pl.BlockSpec(memory_space=m) for m in (pltpu.VMEM, pltpu.HBM))
    labeled = jax.ShapeDtypeStruct((LABELS, wide, depth), jnp.bfloat16)
    a, w = pl.pallas_call(
        functools.partial(pack_kernel, n_tiles, slots, n_amp, grain),
        out_shape=(labeled, labeled),
        in_specs=[hbm] * 4,
        out_specs=(vmem, vmem),
        scratch_shapes=[
            pltpu.VMEM((k_local, width, rows), jnp.bfloat16),
            pltpu.VMEM((LABELS, k_local, width, rows), jnp.bfloat16),
            pltpu.VMEM((rows, depth), jnp.bfloat16),
            pltpu.SMEM(occ_irrep.shape, jnp.int32),
            pltpu.SMEM(tile_irrep.shape, jnp.int32),
            pltpu.SMEM((LABELS * slots,), jnp.int32),
            pltpu.SMEM((LABELS,), jnp.int32),
            pltpu.SemaphoreType.DMA((3,)),
            pltpu.SemaphoreType.DMA((LABELS,)),
        ],
        compiler_params=pltpu.CompilerParams(vmem_limit_bytes=40 * 2**20),
        name="pack",
    )(*(pltpu.with_memory_space_constraint(x, pltpu.HBM) for x in (jnp.swapaxes(amplitudes, 1, 2), integrals, occ_irrep, tile_irrep)))

    share = rows // (n_amp * n_own)
    n_y, n_hi, n_lo = split_of(n_amp, n_own)
    n_flat = n_y * n_lo
    bufs = []
    for lanes, leads in (
        (wide - LANES, ((n_flat - 1, n_hi), (n_hi - 1,))),
        (LANES, ((n_hi - 1, n_flat), (n_flat - 1,))),
    ):
        for lead in leads:
            bufs += [pltpu.VMEM(lead + (share, lanes), jnp.int16)] * 2
            bufs += [pltpu.VMEM(lead + (1, lanes), jnp.float32)] * 2
            bufs += [pltpu.SemaphoreType.DMA((2, lead[0], 3))] * 2
    return pl.pallas_call(
        functools.partial(cycle_kernel, n_y, n_hi, n_lo, slots),
        out_shape=jax.ShapeDtypeStruct((share, rows), jnp.bfloat16),
        in_specs=[vmem, vmem, hbm, hbm],
        out_specs=vmem,
        scratch_shapes=[
            pltpu.VMEM((LABELS, slots, TILE, wide), jnp.float32),
            pltpu.VMEM((n_y, rows // n_y, wide) if share % 8 == 0 else (n_y, 2 * n_own, share, wide), jnp.float32),
            pltpu.VMEM((n_y, n_own, share, wide), jnp.int16),
            pltpu.VMEM((n_y, n_own, share, wide), jnp.int16),
            pltpu.VMEM((n_y, n_own, 1, wide), jnp.float32),
            pltpu.VMEM((n_y, n_own, 1, wide), jnp.float32),
            pltpu.VMEM((wide // LANES, share, LANES), jnp.float32),
            pltpu.VMEM((2, wide // LANES, share, LANES), jnp.float32),
            pltpu.SMEM(occ_irrep.shape, jnp.int32),
            pltpu.SMEM(tile_irrep.shape, jnp.int32),
            pltpu.SMEM((n_tiles,), jnp.int32),
            pltpu.SemaphoreType.DMA((2,)),
            pltpu.SemaphoreType.DMA((2, n_y)),
            pltpu.SemaphoreType.DMA((2, n_y)),
        ]
        + bufs,
        compiler_params=pltpu.CompilerParams(collective_id=0, has_side_effects=True, vmem_limit_bytes=40 * 2**20),
        name="cycle",
    )(a, w, *(pltpu.with_memory_space_constraint(x, pltpu.HBM) for x in (occ_irrep, tile_irrep)))


def solution(mesh):
    return jax.shard_map(
        shards,
        mesh=mesh,
        in_specs=(P("own", None, "amp"), P("own", None, None), P(), P()),
        out_specs=P(("amp", "own"), None),
        check_vma=False,
    )
```

```python
import functools

import jax
import jax.numpy as jnp
from jax import lax
from jax.experimental import pallas as pl
from jax.experimental.pallas import tpu as pltpu
from jax.sharding import PartitionSpec as P

TILE = 64
NI = 2
LABELS = 8
LANES = 128
LEVELS = 32767.0
LEAST = 1e-30
MESH = pl.DeviceIdType.MESH


def gcd(a, b):
    return a if b == 0 else gcd(b, a % b)


def pack_kernel(n_tiles, slots, n_amp, grain, amp_hbm, int_hbm, occ_hbm, tile_hbm, a_ref, w_ref, amp_ref, int_ref, turn_ref, occ_ref, tile_ref, tile_of, count, small_sems, sems):
    k_local, width, rows = amp_ref.shape
    depth = a_ref.shape[2]
    amp_index = lax.axis_index("amp")
    own_index = lax.axis_index("own")

    tile_copy = pltpu.make_async_copy(tile_hbm, tile_ref, small_sems.at[0])
    occ_copy = pltpu.make_async_copy(occ_hbm, occ_ref, small_sems.at[1])
    amp_copy = pltpu.make_async_copy(amp_hbm, amp_ref, small_sems.at[2])
    tile_copy.start()
    occ_copy.start()
    amp_copy.start()
    for i in range(LABELS):
        count[i] = 0
        for s in range(slots):
            tile_of[i * slots + s] = -1
    tile_copy.wait()
    for t in range(n_tiles):
        lab = tile_ref[t]
        rank = count[lab]
        tile_of[lab * slots + rank] = t
        count[lab] = rank + 1
    occ_copy.wait()
    k_lab = [occ_ref[NI + own_index * k_local + k] for k in range(k_local)]

    heads = sorted({min(width, TILE - at * width % TILE) for at in range(n_amp)})
    head_here = jnp.minimum(width, TILE - amp_index * width % TILE)

    def tile_at(lab, k, row):
        at = amp_index * width + row
        return tile_of[jnp.bitwise_xor(lab, k_lab[k]) * slots + at // TILE], at % TILE

    for head in heads:

        @pl.when(head_here == head)
        def _():
            def fetch(lab, carry):
                for k in range(k_local):
                    for row, size in ((0, head), (head, width - head)):
                        if size:
                            t, at = tile_at(lab, k, row)
                            start = pl.multiple_of(jnp.where(t < 0, lab, t) * TILE + at, grain)
                            to = int_ref.at[lab, k, pl.ds(row, size), :]
                            pltpu.make_async_copy(int_hbm.at[k, pl.ds(start, size), :], to, sems.at[lab]).start()
                return carry

            lax.fori_loop(0, LABELS, fetch, 0)

    low = lax.broadcasted_iota(jnp.int32, (width, LANES), 1) < TILE
    row = lax.broadcasted_iota(jnp.int32, (width, LANES), 0)

    def turned(parts):
        spare = depth - k_local * width
        if spare:
            parts = parts + [jnp.zeros((spare, LANES), a_ref.dtype)]
        return jnp.concatenate(parts, axis=0).T

    amp_copy.wait()

    def turn(m, carry):
        at = pl.ds(pl.multiple_of(m * LANES, LANES), LANES)
        turn_ref[at, :] = turned([amp_ref[k, :, at] for k in range(k_local)])
        return carry

    lax.fori_loop(0, rows // LANES, turn, 0, unroll=3)

    def block(lab, carry):
        pltpu.make_async_copy(int_hbm.at[:, pl.ds(0, width), :], int_ref.at[lab], sems.at[lab]).wait()
        held = []
        for k in range(k_local):
            there = [jnp.where(tile_at(lab, k, at)[0] >= 0, 1, 0) for at in (0, width - 1)]
            held.append(jnp.where(row < head_here, there[0], there[1]) > 0)
        zero = jnp.zeros((width, LANES), w_ref.dtype)
        tiles = []
        for q in range(NI * slots):
            i, j = q // slots, q % slots
            tiles.append(i * n_tiles + jnp.maximum(tile_of[jnp.bitwise_xor(lab, occ_ref[i]) * slots + j], 0))
        for q, u in enumerate(tiles):
            a_ref[lab, q * TILE : (q + 1) * TILE, :] = turn_ref[pl.ds(pl.multiple_of(u * TILE, TILE), TILE), :]
        for q in range(0, NI * slots, 2):
            both = []
            for h in range(2):
                u = tiles[q + h]
                at = pl.ds(pl.multiple_of(u // 2 * LANES, LANES), LANES)
                both.append([pltpu.roll(int_ref[lab, k, :, at], (u + h) % 2 * TILE, 1) for k in range(k_local)])
            w_ref[lab, q * TILE : (q + 2) * TILE, :] = turned([jnp.where(here, jnp.where(low, *pair), zero) for here, *pair in zip(held, *both)])
        return carry

    lax.fori_loop(0, LABELS, block, 0)


def split_of(n_amp, n_own):
    lo = 2 if n_own <= 8 else 8
    return n_amp // 2, n_own // lo, lo


def cycle_kernel(n_y, n_hi, n_lo, slots, a_ref, w_ref, occ_hbm, tile_hbm, out_ref, s_ref, x_ref, near_q, near_got, near_m, near_got_m, fin_ref, both_ref, occ_ref, tile_ref, rank_ref, small_sems, near_send, near_recv, *bufs):
    n_own = n_hi * n_lo
    share = fin_ref.shape[1]
    n_tiles = tile_ref.shape[0]
    half = slots * TILE
    wide = NI * half
    amp, own = lax.axis_index("amp"), lax.axis_index("own")
    y, core, hi, lo = amp // 2, amp % 2, own // n_lo, own % n_lo
    n_flat = n_y * n_lo
    split = wide - LANES
    parts = [(0, split), (split, wide)]
    cuts = [[(1, n_hi - 1), (0, 1)], [(n_lo, n_lo), (1, n_lo - 1), (0, 1)] if n_y == 2 else [(1, n_flat - 1), (0, 1)]]
    other = (y * 2 + 1 - core, own)

    def at_of(flat, high):
        return (y + flat // n_lo) % n_y, (hi + high) % n_hi, (lo + flat % n_lo) % n_lo

    def id_of(flat, high):
        y_at, hi_at, lo_at = at_of(flat, high)
        return (y_at * 2 + core, hi_at * n_lo + lo_at)

    tile_copy = pltpu.make_async_copy(tile_hbm, tile_ref, small_sems.at[0])
    occ_copy = pltpu.make_async_copy(occ_hbm, occ_ref, small_sems.at[1])
    tile_copy.start()
    occ_copy.start()
    barrier = pltpu.get_barrier_semaphore()
    pl.semaphore_signal(barrier, inc=1, device_id=other, device_id_type=MESH)
    for j in range(1, n_flat):
        back = (n_y - j // n_lo) % n_y * n_lo + (n_lo - j % n_lo) % n_lo
        pl.semaphore_signal(barrier, inc=1, device_id=id_of(back, 0), device_id_type=MESH)
    for j in range(1, n_hi):
        pl.semaphore_signal(barrier, inc=1, device_id=id_of(0, n_hi - j), device_id_type=MESH)

    def coded(x):
        most = jnp.maximum(jnp.max(jnp.abs(x), axis=0, keepdims=True), LEAST)
        return jnp.round(x * (LEVELS / most)).astype(jnp.int32).astype(jnp.int16), most * (1.0 / LEVELS)

    def plain(q, m):
        return q.astype(jnp.int32).astype(jnp.float32) * m

    def remote(src, dst, send, recv, to):
        return pltpu.make_async_remote_copy(src_ref=src, dst_ref=dst, send_sem=send, recv_sem=recv, device_id=to, device_id_type=MESH)

    def near(y_at, parts_of=(0, 1)):
        return [
            remote(src.at[y_at, :, :, slice(*parts[p])], dst.at[y_at, :, :, slice(*parts[p])], near_send.at[2 * p + which, y_at], near_recv.at[2 * p + which, y_at], other)
            for p in parts_of
            for which, (src, dst) in enumerate(((near_m, near_got_m), (near_q, near_got)))
        ]

    def block(y_at, core_at, own_at, lanes):
        at = core_at * n_own + own_at
        if len(x_ref.shape) == 4:
            return x_ref[y_at, at, :, lanes]
        return x_ref[y_at, pl.ds(pl.multiple_of(at * share, 8), share), lanes]

    def multiply(i):
        rows = pl.ds(pl.multiple_of(i * half, TILE), half)
        over = (((1,), (1,)), ((), ()))

        def step(lab, carry):
            s = lax.dot_general(a_ref[lab, rows, :], w_ref[lab], over, preferred_element_type=jnp.float32)
            s = s + lax.dot_general(w_ref[lab, rows, :], a_ref[lab], over, preferred_element_type=jnp.float32)
            s_ref[lab] = s.reshape(s_ref.shape[1:])
            return carry

        lax.fori_loop(0, LABELS, step, 0, unroll=4)

    def spread(y_at, i):
        count = NI * n_tiles // n_y
        for n in range(count):
            t = y_at * count + n - i * n_tiles
            lab = jnp.bitwise_xor(occ_ref[i], tile_ref[t])
            rank = rank_ref[t]
            if len(x_ref.shape) == 3:
                x_ref[y_at, n * TILE : (n + 1) * TILE] = s_ref[lab, rank]
                continue
            tile = s_ref[lab, rank]
            for b in range(n * TILE // share, -(-(n + 1) * TILE // share)):
                low, high = max(n * TILE, b * share), min((n + 1) * TILE, (b + 1) * share)
                x_ref[y_at, b, low - b * share : high - b * share] = tile[low - n * TILE : high - n * TILE]

        def step(b, carry):
            near_q[y_at, b], near_m[y_at, b] = coded(block(y_at, 1 - core, b, slice(None)))
            return carry

        lax.fori_loop(0, n_own, step, 0, unroll=4)

    def pair(p, flat, high):
        y_at, hi_at, lo_at = at_of(flat, high)
        own_at = hi_at * n_lo + lo_at
        lanes = slice(*parts[p])
        return block(y_at, core, own_at, lanes) + plain(near_got[y_at, own_at, :, lanes], near_got_m[y_at, own_at, :, lanes])

    def far(p, s, j, cut):
        q_send, q_got, m_send, m_got, send, recv = bufs[12 * p + 6 * s :][:6]
        to = id_of(j, 0) if p == s else id_of(0, j)
        at = (j - 1,) if s else (j - 1, pl.ds(cuts[p][cut][0], cuts[p][cut][1]))
        return [
            remote(src.at[at], dst.at[at], send.at[which, j - 1, cut], recv.at[which, j - 1, cut], to)
            for which, (src, dst) in enumerate(((m_send, m_got), (q_send, q_got)))
        ]

    def first(p, cut, partners):
        q_send, _, m_send = bufs[12 * p :][:3]
        start, count = cuts[p][cut]
        for j in partners:
            for i in range(start, start + count):
                q_send[j - 1, i], m_send[j - 1, i] = coded(pair(0, j, i) if p == 0 else pair(1, i, j))
            for copy in far(p, 0, j, cut):
                copy.start()

    def total(p, i):
        _, q_got, _, m_got = bufs[12 * p :][:4]
        x = pair(p, 0, i) if p == 0 else pair(p, i, 0)
        for j in range(q_got.shape[0]):
            x = x + plain(q_got[j, i], m_got[j, i])
        return x

    def keep(p, x):
        for c in range((parts[p][1] - parts[p][0]) // LANES):
            fin_ref[parts[p][0] // LANES + c] = x[:, c * LANES : (c + 1) * LANES]

    def second(p, cut):
        q_send, _, m_send = bufs[12 * p + 6 :][:3]
        for j in range(cuts[p][cut][0], sum(cuts[p][cut])):
            q_send[j - 1], m_send[j - 1] = coded(total(p, j))
            for copy in far(p, 1, j, 0):
                copy.start()

    def last(p, x):
        _, q_got, _, m_got = bufs[12 * p + 6 :][:4]
        for j in range(q_got.shape[0]):
            x = x + plain(q_got[j], m_got[j])
        keep(p, x)

    if n_y == 2:
        stages = [([1], [(1 - y, 1 - y)]), ([0], [(y, y)])]
    else:
        stages = [(list(range(n_y)), [(y_at, y_at * NI // n_y) for y_at in range(n_y)])]

    done = None
    ready = False
    for _, work in stages:
        for y_at, i in work:
            if done is None or n_y == 2 or done != i:
                multiply(i)
                done = i
            if not ready:
                ready = True
                tile_copy.wait()
                occ_copy.wait()
                for t in range(n_tiles):
                    rank = jnp.int32(0)
                    for before in range(t):
                        rank = rank + jnp.where(tile_ref[before] == tile_ref[t], 1, 0)
                    rank_ref[t] = jnp.minimum(rank, slots - 1)
                spread(y_at, i)
                pl.semaphore_wait(barrier, n_flat + n_hi - 1)
            else:
                spread(y_at, i)
            for copy in near(y_at):
                copy.start()
    def received(p, s, cut):
        for j in range(1, n_flat if p == s else n_hi):
            for copy in far(p, s, j, cut):
                copy.wait_recv()

    def left(p, s, cut):
        for j in range(1, n_flat if p == s else n_hi):
            for copy in far(p, s, j, cut):
                copy.wait_send()

    def near_done(work, p):
        for y_at, _ in work:
            for copy in near(y_at, (p,)):
                copy.wait_recv()

    near_done(stages[0][1], 0)
    if n_y == 2:
        first(0, 0, range(n_flat - 1, n_lo - 1, -1))
        near_done(stages[0][1], 1)
        first(1, 0, range(1, n_hi))
        near_done(stages[1][1], 0)
        first(0, 0, range(1, n_lo))
        near_done(stages[1][1], 1)
        first(1, 1, range(1, n_hi))
    else:
        first(0, 0, range(1, n_flat))
        near_done(stages[0][1], 1)
        first(1, 0, range(1, n_hi))
    first(0, 1, range(1, n_flat))
    first(1, len(cuts[1]) - 1, range(1, n_hi))
    for p in range(2):
        for cut in range(len(cuts[p]) - 1):
            received(p, 0, cut)
            second(p, cut)
    kept = []
    for p in range(2):
        received(p, 0, len(cuts[p]) - 1)
        kept.append(total(p, 0))
    for _, work in stages:
        for y_at, _ in work:
            for copy in near(y_at):
                copy.wait_send()
    for p in range(2):
        for cut in range(len(cuts[p])):
            left(p, 0, cut)
    for p in range(2):
        left(p, 1, 0)
    for p in range(2):
        received(p, 1, 0)
        last(p, kept[p])
    expand((amp * n_own + own) * share, slots, fin_ref, both_ref, occ_ref, tile_ref, rank_ref, out_ref)


def expand(base, slots, x_ref, both_ref, occ_ref, tile_ref, rank_ref, out_ref):
    share = x_ref.shape[1]
    n_tiles = tile_ref.shape[0]
    count = NI * n_tiles
    labs = [jnp.bitwise_xor(occ_ref[u // n_tiles], tile_ref[u % n_tiles]) for u in range(count)]

    def label(u):
        return jnp.bitwise_xor(occ_ref[u // n_tiles], tile_ref[u % n_tiles])

    first = base // TILE
    row = base + lax.broadcasted_iota(jnp.int32, (share, LANES), 0)
    low = lax.broadcasted_iota(jnp.int32, (share, LANES), 1) < TILE
    row_lab = jnp.where(row < (first + 1) * TILE, label(first), label(jnp.minimum(first + 1, count - 1)))
    for c in range(x_ref.shape[0]):
        both_ref[0, c] = x_ref[c]
        both_ref[1, c] = pltpu.roll(x_ref[c], TILE, 1)
    for u in range(0, count, 2):
        slot = [(u + h) // n_tiles * slots + rank_ref[(u + h) % n_tiles] for h in range(2)]
        turned = [both_ref[(at + h) % 2, at // 2] for h, at in enumerate(slot)]
        match = row_lab == jnp.where(low, labs[u], labs[u + 1])
        out_ref[:, u * TILE : (u + 2) * TILE] = jnp.where(match, jnp.where(low, *turned), 0.0).astype(out_ref.dtype)


def shards(amplitudes, integrals, occ_irrep, tile_irrep):
    n_amp = lax.axis_size("amp")
    n_own = lax.axis_size("own")
    k_local, rows, width = amplitudes.shape
    n_tiles = tile_irrep.shape[0]
    slots = width * n_amp // TILE
    grain = gcd(width, TILE)
    wide = NI * slots * TILE
    depth = -(-k_local * width // LANES) * LANES
    vmem, hbm = (pl.BlockSpec(memory_space=m) for m in (pltpu.VMEM, pltpu.HBM))
    labeled = jax.ShapeDtypeStruct((LABELS, wide, depth), jnp.bfloat16)
    a, w = pl.pallas_call(
        functools.partial(pack_kernel, n_tiles, slots, n_amp, grain),
        out_shape=(labeled, labeled),
        in_specs=[hbm] * 4,
        out_specs=(vmem, vmem),
        scratch_shapes=[
            pltpu.VMEM((k_local, width, rows), jnp.bfloat16),
            pltpu.VMEM((LABELS, k_local, width, rows), jnp.bfloat16),
            pltpu.VMEM((rows, depth), jnp.bfloat16),
            pltpu.SMEM(occ_irrep.shape, jnp.int32),
            pltpu.SMEM(tile_irrep.shape, jnp.int32),
            pltpu.SMEM((LABELS * slots,), jnp.int32),
            pltpu.SMEM((LABELS,), jnp.int32),
            pltpu.SemaphoreType.DMA((3,)),
            pltpu.SemaphoreType.DMA((LABELS,)),
        ],
        compiler_params=pltpu.CompilerParams(vmem_limit_bytes=40 * 2**20),
        name="pack",
    )(*(pltpu.with_memory_space_constraint(x, pltpu.HBM) for x in (jnp.swapaxes(amplitudes, 1, 2), integrals, occ_irrep, tile_irrep)))

    share = rows // (n_amp * n_own)
    n_y, n_hi, n_lo = split_of(n_amp, n_own)
    n_flat = n_y * n_lo
    bufs = []
    for lanes, leads in (
        (wide - LANES, ((n_flat - 1, n_hi), (n_hi - 1,))),
        (LANES, ((n_hi - 1, n_flat), (n_flat - 1,))),
    ):
        for lead in leads:
            bufs += [pltpu.VMEM(lead + (share, lanes), jnp.int16)] * 2
            bufs += [pltpu.VMEM(lead + (1, lanes), jnp.float32)] * 2
            bufs += [pltpu.SemaphoreType.DMA((2, lead[0], 3))] * 2
    return pl.pallas_call(
        functools.partial(cycle_kernel, n_y, n_hi, n_lo, slots),
        out_shape=jax.ShapeDtypeStruct((share, rows), jnp.bfloat16),
        in_specs=[vmem, vmem, hbm, hbm],
        out_specs=vmem,
        scratch_shapes=[
            pltpu.VMEM((LABELS, slots, TILE, wide), jnp.float32),
            pltpu.VMEM((n_y, rows // n_y, wide) if share % 8 == 0 else (n_y, 2 * n_own, share, wide), jnp.float32),
            pltpu.VMEM((n_y, n_own, share, wide), jnp.int16),
            pltpu.VMEM((n_y, n_own, share, wide), jnp.int16),
            pltpu.VMEM((n_y, n_own, 1, wide), jnp.float32),
            pltpu.VMEM((n_y, n_own, 1, wide), jnp.float32),
            pltpu.VMEM((wide // LANES, share, LANES), jnp.float32),
            pltpu.VMEM((2, wide // LANES, share, LANES), jnp.float32),
            pltpu.SMEM(occ_irrep.shape, jnp.int32),
            pltpu.SMEM(tile_irrep.shape, jnp.int32),
            pltpu.SMEM((n_tiles,), jnp.int32),
            pltpu.SemaphoreType.DMA((2,)),
            pltpu.SemaphoreType.DMA((4, n_y)),
            pltpu.SemaphoreType.DMA((4, n_y)),
        ]
        + bufs,
        compiler_params=pltpu.CompilerParams(collective_id=0, has_side_effects=True, vmem_limit_bytes=40 * 2**20),
        name="cycle",
    )(a, w, *(pltpu.with_memory_space_constraint(x, pltpu.HBM) for x in (occ_irrep, tile_irrep)))


def solution(mesh):
    return jax.shard_map(
        shards,
        mesh=mesh,
        in_specs=(P("own", None, "amp"), P("own", None, None), P(), P()),
        out_specs=P(("amp", "own"), None),
        check_vma=False,
    )
```
